256 devices in a mesh: seq: 8 (over z), dp: 32 (over x, y, core).
Axes of the slice: x: 4, y: 4, z: 8, core: 2. Of those that a mesh axis runs over, the one named last changes fastest.
Arguments:
- tokens: bfloat16 [32, 2048, 1408], P('dp', 'seq'), may hold values from -16 to 16
- weights: bfloat16 [1408, 4, 704], P('dp'), may hold values from -2 to 2
- cotangent: bfloat16 [32, 2048, 1408], P('dp', 'seq'), may hold values from -3 to 3
- col_list: int32 [32, 16, 5], P('dp'), may hold values from 0 to 15, as said below
- cut_lengths: int32 [32, 5], P('dp'), may hold values from 1 to 6, 16 in all within a row
- keep_mask: int32 [32, 2048], P('dp'), may hold values 0 or 1
Outputs:
- sublayer_out: bfloat16 [32, 2048, 1408], P('dp', 'seq')
- grad_tokens: bfloat16 [32, 2048, 1408], P('dp', 'seq')
- grad_weights: float32 [1408, 4, 704], P('dp')
The draws below stay inside these ranges and needn't reach their ends.
Inputs may be any that keep to these rules, and one draw needn't show every extreme that they name: `col_list`: row b lists 5 distinct blocks: b itself first, then blocks within 3 of b, counted cyclically over the packed sequence.
All inputs are finite; a program needn't handle non-finite values. No bound on the sum of `keep_mask` on one device may be relied on, other than what follows from the above.
Results may differ from the reference program's by a relative error of at most 0.038.
Values may be sent and summed in bfloat16 or wider, within the bound.
A program may use at most 128 MiB of HBM per device.

```python
import math
import jax
import jax.numpy as jnp
import numpy as np
from jax import lax

D = 1408
HD = 88
HEADS = 8
HH = 704
NNZ = 5
WIN = 3
SEQLEN = 2048
NBLK = 16
NCUT = 5
MAXCUT = 6
N_DP = 32


def draw_tokens(key, part):
    shape = (N_DP, SEQLEN, D)
    return jnp.clip(jax.random.normal(key, shape, jnp.float32), -6.0, 6.0).astype(jnp.bfloat16)


def draw_weights(key, part):
    key_a, key_b = jax.random.split(key, 2)
    inner = jnp.clip(jax.random.normal(key_a, (D, 3, HH), jnp.float32), -6.0, 6.0) * D ** (-0.5)
    outer = jnp.clip(jax.random.normal(key_b, (D, 1, HH), jnp.float32), -6.0, 6.0) * HH ** (-0.5)
    return jnp.concatenate([inner, outer], axis=1).astype(jnp.bfloat16)


def draw_col_list(key, part):
    rows = N_DP * NBLK
    keys_many = jax.random.split(key, rows)
    orders = jax.vmap(lambda single: jax.random.permutation(single, 2 * WIN))(keys_many).astype(jnp.int32)
    offsets = jnp.where(orders < WIN, orders - WIN, orders - WIN + 1)[:, :NNZ - 1]
    offsets = offsets.reshape(N_DP, NBLK, NNZ - 1)
    blocks = jnp.broadcast_to(jnp.arange(NBLK, dtype=jnp.int32)[None, :, None], (N_DP, NBLK, 1))
    others = (blocks + offsets + NBLK) % NBLK
    return jnp.concatenate([blocks, others], axis=2).astype(jnp.int32)


def place_ends(values, own_key, smallest, high):
    index_at = [jax.random.randint(jax.random.fold_in(own_key, axis), (), 0, length) for axis, length in enumerate(values.shape)]
    longest = values.shape.index(max(values.shape))
    beside = index_at[:longest] + [(index_at[longest] + 1) % values.shape[longest]] + index_at[longest + 1:]
    return values.at[tuple(index_at)].set(smallest).at[tuple(beside)].set(high)


def strengthened(entries, key, source, target, shards_of, factor):
    owner, partner = [(jnp.arange(entries.shape[axis_at]) // (entries.shape[axis_at] // shards_of)).reshape([-1 if axis == axis_at else 1 for axis in range(entries.ndim)]) for axis_at in (source, target)]
    chosen = jax.random.permutation(key, shards_of)[partner]
    strong = (owner == chosen) | (owner == (partner + shards_of // 2) % shards_of)
    return jnp.where(strong, factor * entries, entries)


def levels(own_key, shape, shards, smallest, high):
    factor_of, own = 1.0, jax.random.fold_in(own_key, 6)
    for position, shards_of in shards:
        steps = jnp.exp(jax.random.uniform(jax.random.fold_in(own, position), (shards_of,), jnp.float32, smallest / len(shards), high / len(shards)))
        factor_of = factor_of * jnp.repeat(steps, shape[position] // shards_of).reshape([-1 if axis == position else 1 for axis in range(len(shape))])
    return factor_of


def split_up(number_of, total, limit, slope):
    portions = [(1 << 20) // math.isqrt(standing ** slope) + 1 for standing in range(2, number_of + 1)]
    rest, counts = total - limit - (number_of - 1), [1] * (number_of - 1)
    while rest > 0:
        movable = [i for i in range(number_of - 1) if counts[i] < limit]
        pool, budget = sum([portions[i] for i in movable]), rest
        for i in movable:
            extra = min(limit - counts[i], max(1, budget * portions[i] // pool), rest)
            counts[i] = counts[i] + extra
            rest = rest - extra
    return np.array([limit] + counts)


def uneven(stream_key, number_of, total, bound, slope):
    if number_of == 2:
        one = jax.random.randint(stream_key, (), max(1, total - bound), min(bound, total - 1) + 1)
        return jnp.stack([one, total - one])
    sizes = jnp.asarray(split_up(number_of, total, bound, slope), jnp.int32)
    twos = (number_of - 1) // 2
    donor, sink = sizes[1:1 + 2 * twos:2], sizes[2:2 + 2 * twos:2]
    room = jnp.minimum(donor - 1, bound - sink)
    shifted = jax.random.randint(jax.random.fold_in(stream_key, 1), (twos,), 0, 1 << 20) % (room + 1)
    sizes = sizes.at[1:1 + 2 * twos:2].set(donor - shifted).at[2:2 + 2 * twos:2].set(sink + shifted)
    return sizes[jax.random.permutation(jax.random.fold_in(stream_key, 2), number_of)]


def bell_draw_with(key, shape, deviation, reach, shards, heavy, held_as=jnp.bfloat16):
    array = deviation * jax.random.normal(key, shape, jnp.float32)
    if shards:
        array = array * levels(key, shape, shards, -0.22, 0.18)
    return jnp.clip(strengthened(array, jax.random.fold_in(key, 3), *heavy), -reach, reach).astype(held_as)


def setup_inputs(seed: int = 0) -> dict:
    splits = jax.random.split(jax.random.key(seed), 7)
    tokens = draw_tokens(jax.random.fold_in(splits[6], 71), 0)
    weights = draw_weights(jax.random.fold_in(splits[6], 71), 0)
    cotangent = bell_draw_with(splits[2], (N_DP, SEQLEN, D), 0.5, 3.0, ((0, 32), (1, 8)), (0, 2, 32, 2.75))
    col_list = draw_col_list(jax.random.fold_in(splits[6], 71), 0)
    cut_lengths = jax.vmap(lambda own: uneven(own, NCUT, NBLK, MAXCUT, 2))(jax.random.split(splits[4], N_DP)).reshape((N_DP, NCUT)).astype(jnp.int32)
    keep_mask = place_ends((jax.random.randint(splits[5], (N_DP, SEQLEN), 0, 4) < 3).astype(jnp.int32), jax.random.fold_in(splits[5], 1), 0, 1)
    return dict(tokens=tokens, weights=weights, cotangent=cotangent, col_list=col_list, cut_lengths=cut_lengths, keep_mask=keep_mask)


def block_owner(lengths, count):
    ends = jnp.cumsum(lengths, dtype=jnp.int32)
    index = jnp.arange(count, dtype=jnp.int32)
    return lax.optimization_barrier(jnp.sum((ends[None, :] <= index[:, None]).astype(jnp.int32), axis=1, dtype=jnp.int32))

def allowed_pairs(columns, owner, keep_blocks):
    count, listed = columns.shape
    width = keep_blocks.shape[1]
    same = owner[columns] == owner[:, None]
    kept = keep_blocks[columns] == 1
    itself = columns == jnp.arange(count, dtype=jnp.int32)[:, None]
    diagonal = jnp.eye(width, dtype=bool)
    return same[:, None, :, None] & (kept[:, None, :, :] | itself[:, None, :, None] & diagonal[None, :, None, :])

def attend(query_rows, key_rows, value_rows, columns, allowed, heads):
    length = query_rows.shape[0]
    count = columns.shape[0]
    width = length // count
    scale = 1.0 / math.sqrt(HD)
    query_blk = query_rows.reshape(count, width, heads, HD)
    key_blk = key_rows.reshape(count, width, heads, HD)[columns]
    value_blk = value_rows.reshape(count, width, heads, HD)[columns]
    scores = jnp.einsum('bqhd,bnkhd->bhqnk', query_blk.astype(jnp.float32), key_blk.astype(jnp.float32)) * scale
    scores = jnp.where(allowed[:, None], scores, -jnp.inf)
    largest = lax.optimization_barrier(jnp.max(scores, axis=(3, 4), keepdims=True))
    expd = jnp.exp(scores - largest)
    probs = expd / lax.optimization_barrier(jnp.sum(expd, axis=(3, 4), keepdims=True))
    probs_low = probs.astype(jnp.bfloat16)
    attended = jnp.einsum('bhqnk,bnkhd->bqhd', probs_low.astype(jnp.float32), value_blk.astype(jnp.float32))
    attended = attended.astype(jnp.bfloat16).reshape(length, heads * HD)
    return (attended, probs, probs_low, query_blk, key_blk, value_blk)

def attend_back(d_attended, attended, probs, probs_low, query_blk, key_blk, value_blk, columns):
    count, width, heads, size = query_blk.shape
    scale = 1.0 / math.sqrt(HD)
    d_blk = d_attended.reshape(count, width, heads, size)
    out_blk = attended.reshape(count, width, heads, size)
    delta = lax.optimization_barrier(jnp.sum(d_blk.astype(jnp.float32) * out_blk.astype(jnp.float32), axis=3))
    delta = jnp.transpose(delta, (0, 2, 1))[:, :, :, None, None]
    d_probs = jnp.einsum('bqhd,bnkhd->bhqnk', d_blk.astype(jnp.float32), value_blk.astype(jnp.float32))
    d_scores = (probs * (d_probs - delta) * scale).astype(jnp.bfloat16)
    d_query = jnp.einsum('bhqnk,bnkhd->bqhd', d_scores.astype(jnp.float32), key_blk.astype(jnp.float32))
    d_query = d_query.astype(jnp.bfloat16).reshape(count * width, heads * size)
    d_key_blk = jnp.einsum('bhqnk,bqhd->bnkhd', d_scores.astype(jnp.float32), query_blk.astype(jnp.float32))
    d_value_blk = jnp.einsum('bhqnk,bqhd->bnkhd', probs_low.astype(jnp.float32), d_blk.astype(jnp.float32))
    empty = jnp.zeros((count, width, heads, size), jnp.float32)
    d_key = empty.at[columns].add(d_key_blk).astype(jnp.bfloat16).reshape(count * width, heads * size)
    d_value = empty.at[columns].add(d_value_blk).astype(jnp.bfloat16).reshape(count * width, heads * size)
    return (d_query, d_key, d_value)

def replica(tokens_r, cotangent_r, columns, lengths, keep_r, weights):
    count = columns.shape[0]
    owner = block_owner(lengths, count)
    allowed = allowed_pairs(columns, owner, keep_r.reshape(count, -1))
    inner = weights[:, :3, :].astype(jnp.float32)
    outer = weights[:, 3, :]
    projected = jnp.einsum('td,dch->cth', tokens_r.astype(jnp.float32), inner).astype(jnp.bfloat16)
    attended, probs, probs_low, query_blk, key_blk, value_blk = attend(projected[0], projected[1], projected[2], columns, allowed, HEADS)
    result = jnp.dot(attended, outer.T, preferred_element_type=jnp.float32).astype(jnp.bfloat16)
    d_attended = jnp.dot(cotangent_r, outer, preferred_element_type=jnp.float32).astype(jnp.bfloat16)
    d_query, d_key, d_value = attend_back(d_attended, attended, probs, probs_low, query_blk, key_blk, value_blk, columns)
    d_proj = jnp.stack([d_query, d_key, d_value], axis=0)
    grad_in = jnp.einsum('cth,dch->td', d_proj.astype(jnp.float32), inner).astype(jnp.bfloat16)
    grad_inner = jnp.einsum('td,cth->dch', tokens_r.astype(jnp.float32), d_proj.astype(jnp.float32))
    grad_outer = jnp.dot(cotangent_r.T, attended, preferred_element_type=jnp.float32)
    grad_all = jnp.concatenate([grad_inner, grad_outer[:, None, :]], axis=1)
    return (result, grad_in, grad_all)

def reference(tokens, weights, cotangent, col_list, cut_lengths, keep_mask):

    def step(total, items):
        tokens_r, cotangent_r, columns, lengths, keep_r = items
        result, grad_in, grad_all = replica(tokens_r, cotangent_r, columns, lengths, keep_r, weights)
        return (total + grad_all, (result, grad_in))
    start = jnp.zeros((weights.shape[0], 4, weights.shape[2]), jnp.float32)
    total, stacked = lax.scan(step, start, (tokens, cotangent, col_list, cut_lengths, keep_mask))
    return (stacked[0], stacked[1], total / N_DP)
```

```python
import functools
import math

import jax
import jax.numpy as jnp
from jax import lax
from jax.experimental import pallas as pl
from jax.experimental.pallas import tpu as pltpu
from jax.sharding import PartitionSpec as P

HD = 88
HEADS = 8
HH = 704
D = 1408
BLK = 128
NBLK = 16
NX = 4
NY = 4
NZ = 8
CHIP = 88
CUT = 48
NEG = -1e30
MESH = pl.DeviceIdType.MESH
F32 = jnp.float32
BF16 = jnp.bfloat16
ANY = pl.BlockSpec(memory_space=pl.ANY)
VMEM = pl.BlockSpec(memory_space=pltpu.VMEM)


def place():
    seq = lax.axis_index("seq")
    dp = lax.axis_index("dp")
    return seq, dp // (2 * NY), (dp // 2) % NY, dp % 2


def device(seq, x, y, core):
    return (seq, (x * NY + y) * 2 + core)


def greet(others):
    barrier = pltpu.get_barrier_semaphore()
    for other in others:
        pl.semaphore_signal(barrier, inc=1, device_id=other, device_id_type=MESH)
    pl.semaphore_wait(barrier, len(others))


def neighbours(seq, x, y, core):
    return [
        device(seq, x, y, 1 - core),
        device(seq, (x + 1) % NX, y, core),
        device(seq, (x + NX - 1) % NX, y, core),
        device(seq, x, (y + 1) % NY, core),
        device(seq, x, (y + NY - 1) % NY, core),
    ]


def remote(src, dst, send, recv, target):
    return pltpu.make_async_remote_copy(
        src_ref=src, dst_ref=dst, send_sem=send, recv_sem=recv, device_id=target, device_id_type=MESH
    )


def gather_kernel(
    wpad, tok, wfull, win, sib, blk, loc, sz, rz, sx, rx, s1, r1, s2, r2, ss, rs
):
    seq, x, y, core = place()
    up = (seq + 1) % NZ
    down = (seq + NZ - 1) % NZ
    greet(neighbours(seq, x, y, core) + [device(up, x, y, core), device(down, x, y, core)])

    def rows(first, count):
        return win.at[pl.ds(first * BLK, count * BLK)]

    own_tok = pltpu.make_async_copy(tok, rows(3, 2), loc.at[0])
    own_tok.start()
    to_up = remote(tok, rows(1, 2), sz.at[0], rz.at[0], device(up, x, y, core))
    to_down = remote(tok, rows(5, 2), sz.at[1], rz.at[1], device(down, x, y, core))
    to_up.start()
    to_down.start()
    fwd_up = remote(rows(2, 1), rows(0, 1), sz.at[2], rz.at[2], device(up, x, y, core))
    fwd_down = remote(rows(5, 1), rows(7, 1), sz.at[3], rz.at[3], device(down, x, y, core))

    def weights(c):
        a, b = (x, y) if c == 0 else (y, x)

        def slot(half, aa, bb):
            return wfull.at[half, aa, bb] if c == 0 else wfull.at[half, bb, aa]

        def at(aa, bb):
            return device(seq, aa, bb, c) if c == 0 else device(seq, bb, aa, c)

        other = device(seq, x, y, 1 - c)
        swap = remote(wpad.at[1 - c], sib, sx.at[0], rx.at[0], other)
        swap.start()
        swap.wait_recv()
        blk[...] = wpad[c] + sib[...]
        own = pltpu.make_async_copy(blk, slot(c, a, b), loc.at[1])
        own.start()
        right1, left1 = (a + 1) % 4, (a + 3) % 4
        right2, left2 = (b + 1) % 4, (b + 3) % 4
        opp1, opp2 = (a + 2) % 4, (b + 2) % 4
        part = (pl.ds(0, CUT), pl.ds(CUT, CHIP - CUT))
        sends = [swap]
        order1 = (a, left1, right1, opp1)

        def send(src, dst, ssem, rsem, target):
            copy = remote(src, dst, ssem, rsem, target)
            copy.start()
            sends.append(copy)

        def arrived(dst, ssem, rsem):
            remote(dst, dst, ssem, rsem, other).wait_recv()

        def share(src, index, aa, bb):
            send(src, slot(c, aa, bb), ss.at[index], rs.at[index], other)

        def second(src, k):
            aa = order1[k]
            send(src, slot(c, aa, b), s2.at[k, 0], r2.at[k, 0], at(a, right2))
            send(src, slot(c, aa, b), s2.at[k, 1], r2.at[k, 1], at(a, left2))

        mine = slot(c, a, b)
        send(blk, mine, s1.at[0], r1.at[0], at(right1, b))
        send(blk, mine, s1.at[1], r1.at[1], at(left1, b))
        second(blk, 0)
        share(blk, 0, a, b)
        left_ref, right_ref = slot(c, left1, b), slot(c, right1, b)
        arrived(left_ref, s1.at[0], r1.at[0])
        send(left_ref.at[part[0]], left_ref.at[part[0]], s1.at[2], r1.at[2], at(right1, b))
        second(left_ref, 1)
        share(left_ref, 1, left1, b)
        arrived(right_ref, s1.at[1], r1.at[1])
        send(right_ref.at[part[1]], right_ref.at[part[1]], s1.at[3], r1.at[3], at(left1, b))
        second(right_ref, 2)
        share(right_ref, 2, right1, b)
        to_up.wait_recv()
        fwd_up.start()
        to_down.wait_recv()
        fwd_down.start()
        opp_ref = slot(c, opp1, b)
        arrived(opp_ref.at[part[0]], s1.at[2], r1.at[2])
        arrived(opp_ref.at[part[1]], s1.at[3], r1.at[3])
        second(opp_ref, 3)
        share(opp_ref, 3, opp1, b)
        for k in range(4):
            aa = order1[k]
            from_left, from_right = slot(c, aa, left2), slot(c, aa, right2)
            arrived(from_left, s2.at[k, 0], r2.at[k, 0])
            send(from_left.at[part[0]], from_left.at[part[0]], s2.at[k, 2], r2.at[k, 2], at(a, right2))
            share(from_left, 4 + k, aa, left2)
            arrived(from_right, s2.at[k, 1], r2.at[k, 1])
            send(from_right.at[part[1]], from_right.at[part[1]], s2.at[k, 3], r2.at[k, 3], at(a, left2))
            share(from_right, 8 + k, aa, right2)
        for k in range(4):
            aa = order1[k]
            far = slot(c, aa, opp2)
            arrived(far.at[part[0]], s2.at[k, 2], r2.at[k, 2])
            arrived(far.at[part[1]], s2.at[k, 3], r2.at[k, 3])
            share(far, 12 + k, aa, opp2)
        others1 = (b, (b + 3) % 4, (b + 1) % 4, (b + 2) % 4)
        others2 = (a, (a + 3) % 4, (a + 1) % 4, (a + 2) % 4)
        for j in range(4):
            for k in range(4):
                dst = slot(1 - c, others2[j], others1[k])
                arrived(dst, ss.at[4 * j + k], rs.at[4 * j + k])
        for copy in sends:
            copy.wait_send()
        own.wait()

    @pl.when(core == 0)
    def _():
        weights(0)

    @pl.when(core == 1)
    def _():
        weights(1)

    own_tok.wait()
    fwd_up.wait()
    fwd_down.wait()
    to_up.wait_send()
    to_down.wait_send()


def gather(wpad, tok):
    dma = pltpu.SemaphoreType.DMA
    return pl.pallas_call(
        gather_kernel,
        out_shape=(
            jax.ShapeDtypeStruct((2, NX, NY, CHIP, D), BF16),
            jax.ShapeDtypeStruct((8 * BLK, D), BF16),
        ),
        in_specs=[VMEM, ANY],
        out_specs=(ANY, ANY),
        scratch_shapes=[
            pltpu.VMEM((CHIP, D), BF16),
            pltpu.VMEM((CHIP, D), BF16),
            dma((2,)),
            dma((4,)),
            dma((4,)),
            dma((1,)),
            dma((1,)),
            dma((4,)),
            dma((4,)),
            dma((4, 4)),
            dma((4, 4)),
            dma((16,)),
            dma((16,)),
        ],
        compiler_params=pltpu.CompilerParams(
            collective_id=0, has_side_effects=True, vmem_limit_bytes=16 << 20
        ),
        name="gather_weights_halo",
    )(wpad, tok)


COLS = (0, 384, 768, 1024)
ROWS = (0, 40)


def reduce_kernel(
    g, out, sib, mine, p1, q1, p2, q2, pieces, rz, total, loc, ss, rs, s1, r1, s2, r2, sz, rzs, sg, rg, sw, rw
):
    seq, x, y, core = place()
    peers = [device((seq + k) % NZ, x, y, core) for k in range(1, NZ)]
    greet(neighbours(seq, x, y, core) + peers)

    def run(c):
        a, b = (x, y) if c == 0 else (y, x)

        def slot(ref, aa, bb):
            return ref.at[aa, bb] if c == 0 else ref.at[bb, aa]

        def at(aa, bb):
            return device(seq, aa, bb, c) if c == 0 else device(seq, bb, aa, c)

        other = device(seq, x, y, 1 - c)
        right1, left1, opp1 = (a + 1) % 4, (a + 3) % 4, (a + 2) % 4
        right2, left2, opp2 = (b + 1) % 4, (b + 3) % 4, (b + 2) % 4
        order1 = (opp1, right1, left1, a)
        order2 = (opp2, right2, left2, b)
        part = (pl.ds(0, CUT), pl.ds(CUT, CHIP - CUT))
        sends = []

        def send(src, dst, ssem, rsem, target):
            copy = remote(src, dst, ssem, rsem, target)
            copy.start()
            sends.append(copy)

        def arrived(dst, ssem, rsem):
            remote(dst, dst, ssem, rsem, other).wait_recv()

        locals_ = []
        for j in range(4):
            for k in range(4):
                copy = pltpu.make_async_copy(
                    slot(g.at[c], order1[k], order2[j]), slot(mine, order1[k], order2[j]), loc.at[4 * j + k]
                )
                copy.start()
                locals_.append(copy)
                aa, bb = order2[k], order1[j]
                send(
                    slot(g.at[1 - c], bb, aa),
                    slot(sib, bb, aa),
                    ss.at[4 * j + k],
                    rs.at[4 * j + k],
                    other,
                )

        def add(j, k):
            dst = slot(sib, order1[k], order2[j])
            own = slot(mine, order1[k], order2[j])
            locals_[4 * j + k].wait()
            arrived(dst, ss.at[4 * j + k], rs.at[4 * j + k])
            own[...] = (own[...].astype(F32) + dst[...].astype(F32)).astype(BF16)

        def first(j):
            add(j, 0)
            far = slot(mine, opp1, order2[j])
            send(far.at[part[0]], p1.at[j, part[0]], s1.at[j, 0], r1.at[j, 0], at(right1, b))
            send(far.at[part[1]], p1.at[j, part[1]], s1.at[j, 1], r1.at[j, 1], at(left1, b))
            for k in range(1, 4):
                add(j, k)

        def middle(j):
            near = slot(mine, right1, order2[j])
            arrived(p1.at[j, part[0]], s1.at[j, 0], r1.at[j, 0])
            near[part[0]] = (near[part[0]].astype(F32) + p1[j, part[0]].astype(F32)).astype(BF16)
            send(near, q1.at[j, 0], s1.at[j, 2], r1.at[j, 2], at(right1, b))
            near = slot(mine, left1, order2[j])
            arrived(p1.at[j, part[1]], s1.at[j, 1], r1.at[j, 1])
            near[part[1]] = (near[part[1]].astype(F32) + p1[j, part[1]].astype(F32)).astype(BF16)
            send(near, q1.at[j, 1], s1.at[j, 3], r1.at[j, 3], at(left1, b))

        def last(j):
            own = slot(mine, a, order2[j])
            arrived(q1.at[j, 0], s1.at[j, 2], r1.at[j, 2])
            arrived(q1.at[j, 1], s1.at[j, 3], r1.at[j, 3])
            own[...] = (
                own[...].astype(F32) + q1[j, 0].astype(F32) + q1[j, 1].astype(F32)
            ).astype(BF16)
            if j == 0:
                send(own.at[part[0]], p2.at[part[0]], s2.at[0], r2.at[0], at(a, right2))
                send(own.at[part[1]], p2.at[part[1]], s2.at[1], r2.at[1], at(a, left2))
            elif j == 1:
                arrived(p2.at[part[0]], s2.at[0], r2.at[0])
                own[part[0]] = (own[part[0]].astype(F32) + p2[part[0]].astype(F32)).astype(BF16)
                send(own, q2.at[0], s2.at[2], r2.at[2], at(a, right2))
            elif j == 2:
                arrived(p2.at[part[1]], s2.at[1], r2.at[1])
                own[part[1]] = (own[part[1]].astype(F32) + p2[part[1]].astype(F32)).astype(BF16)
                send(own, q2.at[1], s2.at[3], r2.at[3], at(a, left2))

        for step in range(6):
            if step < 4:
                first(step)
            if 0 <= step - 1 < 4:
                middle(step - 1)
            if 0 <= step - 2 < 4:
                last(step - 2)
        own = slot(mine, a, b)
        arrived(q2.at[0], s2.at[2], r2.at[2])
        arrived(q2.at[1], s2.at[3], r2.at[3])
        total[...] = own[...].astype(F32) + q2[0].astype(F32) + q2[1].astype(F32)
        for piece in range(8):
            r0, c0 = ROWS[piece // 4], COLS[piece % 4]
            pieces[piece] = total[r0 : r0 + 48, c0 : c0 + 384].astype(BF16)
        for k in range(1, NZ):
            target = (seq + k) % NZ
            send(pieces.at[target], rz.at[k - 1], sz.at[k - 1], rzs.at[k - 1], peers[k - 1])
        acc = pieces[seq].astype(F32)
        for k in range(1, NZ):
            arrived(rz.at[k - 1], sz.at[k - 1], rzs.at[k - 1])
            acc = acc + rz[k - 1].astype(F32)
        out[c, seq] = acc.astype(BF16)
        for k in range(1, NZ):
            send(out.at[c, seq], out.at[c, seq], sg.at[k - 1], rg.at[k - 1], peers[k - 1])
        send(out.at[c, seq], out.at[c, seq], sw.at[0], rw.at[0], other)
        for k in range(1, NZ):
            source = (seq + NZ - k) % NZ
            arrived(out.at[c, source], sg.at[k - 1], rg.at[k - 1])
            send(out.at[c, source], out.at[c, source], sw.at[k], rw.at[k], other)
        for k in range(NZ):
            source = (seq + NZ - k) % NZ
            arrived(out.at[1 - c, source], sw.at[k], rw.at[k])
        for copy in sends:
            copy.wait_send()

    @pl.when(core == 0)
    def _():
        run(0)

    @pl.when(core == 1)
    def _():
        run(1)


def reduce_all(g):
    dma = pltpu.SemaphoreType.DMA
    return pl.pallas_call(
        reduce_kernel,
        out_shape=jax.ShapeDtypeStruct((2, NZ, 48, 384), BF16),
        in_specs=[ANY],
        out_specs=VMEM,
        scratch_shapes=[
            pltpu.VMEM((NX, NY, CHIP, D), BF16),
            pltpu.VMEM((NX, NY, CHIP, D), BF16),
            pltpu.VMEM((4, CHIP, D), BF16),
            pltpu.VMEM((4, 2, CHIP, D), BF16),
            pltpu.VMEM((CHIP, D), BF16),
            pltpu.VMEM((2, CHIP, D), BF16),
            pltpu.VMEM((8, 48, 384), BF16),
            pltpu.VMEM((7, 48, 384), BF16),
            pltpu.VMEM((CHIP, D), F32),
            dma((16,)),
            dma((16,)),
            dma((16,)),
            dma((4, 4)),
            dma((4, 4)),
            dma((4,)),
            dma((4,)),
            dma((7,)),
            dma((7,)),
            dma((7,)),
            dma((7,)),
            dma((8,)),
            dma((8,)),
        ],
        compiler_params=pltpu.CompilerParams(
            collective_id=1, has_side_effects=True, vmem_limit_bytes=48 << 20
        ),
        name="reduce_weight_grads",
    )(g)


NT = (((1,), (1,)), ((), ()))
SCALE = 1.0 / math.sqrt(HD)


def dot(lhs, rhs):
    return jnp.dot(lhs, rhs, preferred_element_type=F32)


def dot_t(lhs, rhs):
    return lax.dot_general(lhs, rhs, NT, preferred_element_type=F32)


def split_heads(src, dst, first, rows):
    dst[...] = jnp.zeros_like(dst)
    for h in range(HEADS):
        dst[h, :, 0:HD] = src[rows, first + h * HD : first + (h + 1) * HD]


def forward_kernel(qk, v, da, rowbias, att, dq, stats, qh, kh, vh, dh, oh, gh, bias):
    everything = pl.ds(0, 8 * BLK)
    own = pl.ds(3 * BLK, 2 * BLK)
    split_heads(qk, qh, 0, own)
    split_heads(qk, kh, HH, everything)
    split_heads(v, vh, 0, everything)
    split_heads(da, dh, HH, pl.ds(0, 2 * BLK))
    row = lax.broadcasted_iota(jnp.int32, (BLK, 8 * BLK), 0)
    col = lax.broadcasted_iota(jnp.int32, (BLK, 8 * BLK), 1)
    for i in range(2):
        line = jnp.broadcast_to(rowbias[i : i + 1, :], (BLK, 8 * BLK))
        bias[i] = jnp.where(col == row + (3 + i) * BLK, 0.0, line)
    lane = lax.broadcasted_iota(jnp.int32, (BLK, BLK), 1)
    stats[...] = jnp.zeros_like(stats)

    def head(h, carry):
        for i in range(2):
            mine = slice(i * BLK, (i + 1) * BLK)
            keys = slice(i * BLK, (i + 7) * BLK)
            s = dot_t(qh[h, mine, :], kh[h, keys, :]) * SCALE + bias[i, :, keys]
            top = jnp.max(s, axis=1, keepdims=True)
            e = jnp.exp(s - top)
            norm = jnp.sum(e, axis=1, keepdims=True)
            p = e * (1.0 / norm)
            o = dot(p.astype(BF16), vh[h, keys, :]).astype(BF16)
            oh[h, mine, :] = o
            d = dh[h, mine, :]
            delta = jnp.sum(d.astype(F32) * o.astype(F32), axis=1, keepdims=True)
            dp = dot_t(d, vh[h, keys, :])
            ds = (p * (dp - delta) * SCALE).astype(BF16)
            gh[h, mine, :] = dot(ds, kh[h, keys, :]).astype(BF16)
            old = stats[mine, :]
            lse = top + jnp.log(norm)
            stats[mine, :] = jnp.where(lane == h, lse, jnp.where(lane == h + HEADS, delta, old))
        return carry

    lax.fori_loop(0, HEADS, head, 0)
    for h in range(HEADS):
        att[:, h * HD : (h + 1) * HD] = oh[h, :, 0:HD]
        dq[:, h * HD : (h + 1) * HD] = gh[h, :, 0:HD]


def forward(qk, v, da, rowbias):
    window, own = 8 * BLK, 2 * BLK
    cost = pl.CostEstimate(
        flops=8 * HEADS * own * 7 * BLK * BLK, transcendentals=HEADS * own * window, bytes_accessed=16 << 20
    )
    return pl.pallas_call(
        forward_kernel,
        out_shape=(
            jax.ShapeDtypeStruct((own, HH), BF16),
            jax.ShapeDtypeStruct((own, HH), BF16),
            jax.ShapeDtypeStruct((own, BLK), F32),
        ),
        in_specs=[VMEM] * 4,
        out_specs=(VMEM,) * 3,
        scratch_shapes=[
            pltpu.VMEM((HEADS, own, BLK), BF16),
            pltpu.VMEM((HEADS, window, BLK), BF16),
            pltpu.VMEM((HEADS, window, BLK), BF16),
            pltpu.VMEM((HEADS, own, BLK), BF16),
            pltpu.VMEM((HEADS, own, BLK), BF16),
            pltpu.VMEM((HEADS, own, BLK), BF16),
            pltpu.VMEM((2, BLK, window), F32),
        ],
        compiler_params=pltpu.CompilerParams(vmem_limit_bytes=40 << 20),
        cost_estimate=cost,
        name="attend_queries",
    )(qk, v, da, rowbias)


def backward_kernel(qk, v, da, stats, rowbias, colbias, dk, dv, qh, kh, vh, dh, kg, vg, bias):
    everything = pl.ds(0, 8 * BLK)
    own = pl.ds(3 * BLK, 2 * BLK)
    split_heads(qk, qh, 0, everything)
    split_heads(qk, kh, HH, own)
    split_heads(v, vh, 0, own)
    split_heads(da, dh, 0, everything)
    row = lax.broadcasted_iota(jnp.int32, (BLK, 8 * BLK), 0)
    col = lax.broadcasted_iota(jnp.int32, (BLK, 8 * BLK), 1)
    for i in range(2):
        line = jnp.broadcast_to(rowbias[i : i + 1, :], (BLK, 8 * BLK))
        line = line + colbias[i * BLK : (i + 1) * BLK, :]
        bias[i] = jnp.where(col == row + (3 + i) * BLK, 0.0, line)

    def head(h, carry):
        for i in range(2):
            mine = slice(i * BLK, (i + 1) * BLK)
            asks = slice(i * BLK, (i + 7) * BLK)
            lse = stats[pl.ds(h, 1), asks]
            delta = stats[pl.ds(h + HEADS, 1), asks]
            s = dot_t(kh[h, mine, :], qh[h, asks, :]) * SCALE + bias[i, :, asks]
            p = jnp.exp(s - lse)
            dp = dot_t(vh[h, mine, :], dh[h, asks, :])
            ds = (p * (dp - delta) * SCALE).astype(BF16)
            vg[h, mine, :] = dot(p.astype(BF16), dh[h, asks, :]).astype(BF16)
            kg[h, mine, :] = dot(ds, qh[h, asks, :]).astype(BF16)
        return carry

    lax.fori_loop(0, HEADS, head, 0)
    for h in range(HEADS):
        dk[:, h * HD : (h + 1) * HD] = kg[h, :, 0:HD]
        dv[:, h * HD : (h + 1) * HD] = vg[h, :, 0:HD]


def backward(qk, v, da, stats, rowbias, colbias):
    window, own = 8 * BLK, 2 * BLK
    cost = pl.CostEstimate(
        flops=8 * HEADS * own * 7 * BLK * BLK, transcendentals=HEADS * own * window, bytes_accessed=16 << 20
    )
    return pl.pallas_call(
        backward_kernel,
        out_shape=(
            jax.ShapeDtypeStruct((own, HH), BF16),
            jax.ShapeDtypeStruct((own, HH), BF16),
        ),
        in_specs=[VMEM] * 6,
        out_specs=(VMEM,) * 2,
        scratch_shapes=[
            pltpu.VMEM((HEADS, window, BLK), BF16),
            pltpu.VMEM((HEADS, own, BLK), BF16),
            pltpu.VMEM((HEADS, own, BLK), BF16),
            pltpu.VMEM((HEADS, window, BLK), BF16),
            pltpu.VMEM((HEADS, own, BLK), BF16),
            pltpu.VMEM((HEADS, own, BLK), BF16),
            pltpu.VMEM((2, BLK, window), F32),
        ],
        compiler_params=pltpu.CompilerParams(vmem_limit_bytes=40 << 20),
        cost_estimate=cost,
        name="attend_keys",
    )(qk, v, da, stats, rowbias, colbias)


def biases(columns, lengths, keep):
    seq = lax.axis_index("seq")
    start = (2 * seq + NBLK - 3) % NBLK
    blocks = (start + jnp.arange(8, dtype=jnp.int32)) % NBLK
    mine = 2 * seq + jnp.arange(2, dtype=jnp.int32)
    cut = jnp.arange(lengths.shape[0], dtype=jnp.int32)
    ends = jnp.sum(jnp.where(cut[None, :] <= cut[:, None], lengths[None, :], 0), axis=1)

    def owner(index):
        return jnp.sum((ends[None, :] <= index[:, None]).astype(jnp.int32), axis=1)

    same = owner(mine)[:, None] == owner(blocks)[None, :]
    twice = jnp.concatenate([columns, columns], axis=0)
    columns_mine = lax.dynamic_slice(columns, (2 * seq, 0), (2, columns.shape[1]))
    columns_win = lax.dynamic_slice(twice, (start, 0), (8, columns.shape[1]))
    ask = same & jnp.any(columns_mine[:, None, :] == blocks[None, :, None], axis=2)
    give = same & jnp.any(columns_win[None, :, :] == mine[:, None, None], axis=2)
    kept = keep.reshape(NBLK, BLK)
    kept_win = lax.dynamic_slice(jnp.concatenate([kept, kept], axis=0), (start, 0), (8, BLK))
    kept_mine = lax.dynamic_slice(kept, (2 * seq, 0), (2, BLK))
    ask_rows = jnp.where(ask[:, :, None] & (kept_win == 1)[None], 0.0, NEG).reshape(2, 8 * BLK)
    give_rows = jnp.broadcast_to(jnp.where(give, 0.0, NEG)[:, :, None], (2, 8, BLK)).reshape(2, 8 * BLK)
    give_cols = jnp.where(kept_mine == 1, 0.0, NEG).reshape(2 * BLK, 1)
    return ask_rows.astype(F32), give_rows.astype(F32), give_cols.astype(F32)


def widen(own):
    up = [(i, (i + 1) % NZ) for i in range(NZ)]
    down = [(i, (i + NZ - 1) % NZ) for i in range(NZ)]
    up2 = [(i, (i + 2) % NZ) for i in range(NZ)]
    down2 = [(i, (i + NZ - 2) % NZ) for i in range(NZ)]
    below = lax.ppermute(own, "seq", up)
    above = lax.ppermute(own, "seq", down)
    far_below = lax.ppermute(own[BLK:], "seq", up2)
    far_above = lax.ppermute(own[:BLK], "seq", down2)
    return jnp.concatenate([far_below, below, own, above, far_above], axis=0)


def body(tokens, weights, cotangent, col_list, cut_lengths, keep_mask):
    replicas = lax.axis_size("dp")
    core = lax.axis_index("dp") % 2
    inputs = tokens[0]
    upstream = cotangent[0]
    shard = weights.shape[0]
    halves = jnp.transpose(weights.reshape(shard, 2, D), (1, 0, 2))
    padded = lax.dynamic_update_slice(jnp.zeros((2, CHIP, D), BF16), halves, (0, shard * core, 0))
    full, window = gather(padded, inputs)
    full = full.reshape(2, D, D)
    w_a, w_b = full[0], full[1]
    ask_rows, give_rows, give_cols = biases(col_list[0], cut_lengths[0], keep_mask[0])

    d_att_wide = dot(upstream, w_b).astype(BF16)
    qk = dot(window, w_a).astype(BF16)
    v = dot(window, w_b).astype(BF16)
    d_att_win = widen(d_att_wide[:, HH:])
    attended, d_q, stats = forward(qk, v, d_att_wide, ask_rows)
    stats_win = widen(stats[:, : 2 * HEADS])
    d_k, d_v = backward(qk, v, d_att_win, stats_win.T, give_rows, give_cols)

    zeros = jnp.zeros_like(d_v)
    d_qk = jnp.concatenate([d_q, d_k], axis=1)
    d_v_wide = jnp.concatenate([d_v, zeros], axis=1)
    att_wide = jnp.concatenate([zeros, attended], axis=1)
    result = dot_t(att_wide, w_b).astype(BF16)
    grad_in = (dot_t(d_qk, w_a) + dot_t(d_v_wide, w_b)).astype(BF16)
    g_a = dot(inputs.T, d_qk).astype(BF16)
    g_v = dot(inputs.T, d_v)
    g_o = dot(upstream.T, attended)
    g_b = jnp.concatenate([g_v, g_o], axis=1).astype(BF16)
    parts = jnp.stack([g_a, g_b], axis=0).reshape(2, NX, NY, CHIP, D)
    pieces = reduce_all(parts)
    low = jnp.concatenate([pieces[:, 0], pieces[:, 1], pieces[:, 2, :, :256], pieces[:, 3]], axis=2)
    high = jnp.concatenate([pieces[:, 4], pieces[:, 5], pieces[:, 6, :, :256], pieces[:, 7]], axis=2)
    summed = jnp.concatenate([low[:, :40], high], axis=1)
    mine = lax.dynamic_slice(summed, (0, shard * core, 0), (2, shard, D))
    grad_all = jnp.transpose(mine, (1, 0, 2)).reshape(shard, 4, HH).astype(F32) / replicas
    return (result[None], grad_in[None], grad_all)


def solution(mesh):
    placed = (
        P("dp", "seq", None),
        P("dp", None, None),
        P("dp", "seq", None),
        P("dp", None, None),
        P("dp", None),
        P("dp", None),
    )
    return jax.shard_map(
        body,
        mesh=mesh,
        in_specs=placed,
        out_specs=(P("dp", "seq", None), P("dp", "seq", None), P("dp", None, None)),
        check_vma=False,
    )
```

```python
import functools
import math

import jax
import jax.numpy as jnp
from jax import lax
from jax.experimental import pallas as pl
from jax.experimental.pallas import tpu as pltpu
from jax.sharding import PartitionSpec as P

HD = 88
HEADS = 8
HH = 704
D = 1408
OWN = 256
WINDOW = 1024
BLK = 128
NBLK = 16
NX = 4
NY = 4
NZ = 8
CHIP = 88
CUT = 48
NEG = -1e30
MESH = pl.DeviceIdType.MESH
F32 = jnp.float32
BF16 = jnp.bfloat16
ANY = pl.BlockSpec(memory_space=pl.ANY)
VMEM = pl.BlockSpec(memory_space=pltpu.VMEM)


def place():
    seq = lax.axis_index("seq")
    dp = lax.axis_index("dp")
    return seq, dp // (2 * NY), (dp // 2) % NY, dp % 2


def device(seq, x, y, core):
    return (seq, (x * NY + y) * 2 + core)


def greet(others):
    barrier = pltpu.get_barrier_semaphore()
    for other in others:
        pl.semaphore_signal(barrier, inc=1, device_id=other, device_id_type=MESH)
    pl.semaphore_wait(barrier, len(others))


def neighbours(seq, x, y, core):
    return [
        device(seq, x, y, 1 - core),
        device(seq, (x + 1) % NX, y, core),
        device(seq, (x + NX - 1) % NX, y, core),
        device(seq, x, (y + 1) % NY, core),
        device(seq, x, (y + NY - 1) % NY, core),
    ]


def remote(src, dst, send, recv, target):
    return pltpu.make_async_remote_copy(
        src_ref=src, dst_ref=dst, send_sem=send, recv_sem=recv, device_id=target, device_id_type=MESH
    )


def gather_kernel(
    wpad, tok, wfull, win, sib, blk, loc, sz, rz, sx, rx, s1, r1, s2, r2, ss, rs
):
    seq, x, y, core = place()
    up = (seq + 1) % NZ
    down = (seq + NZ - 1) % NZ
    greet(neighbours(seq, x, y, core) + [device(up, x, y, core), device(down, x, y, core)])

    def rows(first, count):
        return win.at[pl.ds(first * BLK, count * BLK)]

    own_tok = pltpu.make_async_copy(tok, rows(3, 2), loc.at[0])
    own_tok.start()
    low, high = tok.at[pl.ds(0, BLK)], tok.at[pl.ds(BLK, BLK)]
    edge_up = remote(high, rows(2, 1), sz.at[0], rz.at[0], device(up, x, y, core))
    edge_down = remote(low, rows(5, 1), sz.at[1], rz.at[1], device(down, x, y, core))
    to_up = remote(low, rows(1, 1), sz.at[4], rz.at[4], device(up, x, y, core))
    to_down = remote(high, rows(6, 1), sz.at[5], rz.at[5], device(down, x, y, core))
    edge_up.start()
    edge_down.start()
    to_up.start()
    to_down.start()
    fwd_up = remote(rows(2, 1), rows(0, 1), sz.at[2], rz.at[2], device(up, x, y, core))
    fwd_down = remote(rows(5, 1), rows(7, 1), sz.at[3], rz.at[3], device(down, x, y, core))

    def weights(c):
        a, b = (x, y) if c == 0 else (y, x)

        def slot(half, aa, bb):
            return wfull.at[half, :, aa, bb] if c == 0 else wfull.at[half, :, bb, aa]

        def at(aa, bb):
            return device(seq, aa, bb, c) if c == 0 else device(seq, bb, aa, c)

        other = device(seq, x, y, 1 - c)
        swap = remote(wpad.at[1 - c], sib, sx.at[0], rx.at[0], other)
        swap.start()
        swap.wait_recv()
        blk[...] = wpad[c] + sib[...]
        own = pltpu.make_async_copy(blk, slot(c, a, b), loc.at[1])
        own.start()
        right1, left1 = (a + 1) % 4, (a + 3) % 4
        right2, left2 = (b + 1) % 4, (b + 3) % 4
        opp1, opp2 = (a + 2) % 4, (b + 2) % 4
        part = (pl.ds(0, CUT), pl.ds(CUT, CHIP - CUT))
        sends = [swap]
        order1 = (a, left1, right1, opp1)

        def send(src, dst, ssem, rsem, target):
            copy = remote(src, dst, ssem, rsem, target)
            copy.start()
            sends.append(copy)

        def arrived(dst, ssem, rsem):
            remote(dst, dst, ssem, rsem, other).wait_recv()

        def share(src, index, aa, bb):
            send(src, slot(c, aa, bb), ss.at[index], rs.at[index], other)

        def second(src, k):
            aa = order1[k]
            send(src, slot(c, aa, b), s2.at[k, 0], r2.at[k, 0], at(a, right2))
            send(src, slot(c, aa, b), s2.at[k, 1], r2.at[k, 1], at(a, left2))

        mine = slot(c, a, b)
        send(blk, mine, s1.at[0], r1.at[0], at(right1, b))
        send(blk, mine, s1.at[1], r1.at[1], at(left1, b))
        second(blk, 0)
        share(blk, 0, a, b)
        left_ref, right_ref = slot(c, left1, b), slot(c, right1, b)
        arrived(left_ref, s1.at[0], r1.at[0])
        send(left_ref.at[:, part[0]], left_ref.at[:, part[0]], s1.at[2], r1.at[2], at(right1, b))
        second(left_ref, 1)
        share(left_ref, 1, left1, b)
        arrived(right_ref, s1.at[1], r1.at[1])
        send(right_ref.at[:, part[1]], right_ref.at[:, part[1]], s1.at[3], r1.at[3], at(left1, b))
        second(right_ref, 2)
        share(right_ref, 2, right1, b)
        opp_ref = slot(c, opp1, b)
        arrived(opp_ref.at[:, part[0]], s1.at[2], r1.at[2])
        arrived(opp_ref.at[:, part[1]], s1.at[3], r1.at[3])
        second(opp_ref, 3)
        share(opp_ref, 3, opp1, b)
        for k in range(4):
            if k == 3:
                edge_up.wait_recv()
                fwd_up.start()
                edge_down.wait_recv()
                fwd_down.start()
            aa = order1[k]
            from_left, from_right = slot(c, aa, left2), slot(c, aa, right2)
            arrived(from_left, s2.at[k, 0], r2.at[k, 0])
            send(from_left.at[:, part[0]], from_left.at[:, part[0]], s2.at[k, 2], r2.at[k, 2], at(a, right2))
            share(from_left, 4 + k, aa, left2)
            arrived(from_right, s2.at[k, 1], r2.at[k, 1])
            send(from_right.at[:, part[1]], from_right.at[:, part[1]], s2.at[k, 3], r2.at[k, 3], at(a, left2))
            share(from_right, 8 + k, aa, right2)
        for k in range(4):
            aa = order1[k]
            far = slot(c, aa, opp2)
            arrived(far.at[:, part[0]], s2.at[k, 2], r2.at[k, 2])
            arrived(far.at[:, part[1]], s2.at[k, 3], r2.at[k, 3])
            share(far, 12 + k, aa, opp2)
        others1 = (b, (b + 3) % 4, (b + 1) % 4, (b + 2) % 4)
        others2 = (a, (a + 3) % 4, (a + 1) % 4, (a + 2) % 4)
        for j in range(4):
            for k in range(4):
                dst = slot(1 - c, others2[j], others1[k])
                arrived(dst, ss.at[4 * j + k], rs.at[4 * j + k])
        for copy in sends:
            copy.wait_send()
        own.wait()

    @pl.when(core == 0)
    def _():
        weights(0)

    @pl.when(core == 1)
    def _():
        weights(1)

    own_tok.wait()
    fwd_up.wait()
    fwd_down.wait()
    to_up.wait()
    to_down.wait()
    edge_up.wait_send()
    edge_down.wait_send()


def gather(wpad, tok):
    dma = pltpu.SemaphoreType.DMA
    return pl.pallas_call(
        gather_kernel,
        out_shape=(
            jax.ShapeDtypeStruct((2, 2, NX, NY, CHIP, HH), BF16),
            jax.ShapeDtypeStruct((8 * BLK, D), BF16),
        ),
        in_specs=[VMEM, ANY],
        out_specs=(ANY, ANY),
        scratch_shapes=[
            pltpu.VMEM((2, CHIP, HH), BF16),
            pltpu.VMEM((2, CHIP, HH), BF16),
            dma((2,)),
            dma((6,)),
            dma((6,)),
            dma((1,)),
            dma((1,)),
            dma((4,)),
            dma((4,)),
            dma((4, 4)),
            dma((4, 4)),
            dma((16,)),
            dma((16,)),
        ],
        compiler_params=pltpu.CompilerParams(
            collective_id=0, has_side_effects=True, vmem_limit_bytes=16 << 20
        ),
        name="gather_weights_halo",
    )(wpad, tok)


NT = (((1,), (1,)), ((), ()))
SCALE = 1.0 / math.sqrt(HD)
SCALE2 = SCALE * math.log2(math.e)
ROWS = (0, 24, 48, 64)
COLS = (0, 320)


def dot(lhs, rhs):
    return jnp.dot(lhs, rhs, preferred_element_type=F32)


def dot_t(lhs, rhs):
    return lax.dot_general(lhs, rhs, NT, preferred_element_type=F32)


class Wave:
    def __init__(self, refs, sems, seq, x, y, core):
        self.g, self.sib, self.p1, self.q1, self.p2, self.q2, self.pieces, self.rz, self.zz = refs
        self.sems = sems
        self.seq, self.core = seq, core
        self.a, self.b = (1 - core) * x + core * y, (1 - core) * y + core * x
        a, b = self.a, self.b
        self.order1 = ((a + 2) % 4, (a + 1) % 4, (a + 3) % 4, a)
        self.order2 = ((b + 2) % 4, (b + 1) % 4, (b + 3) % 4, b)
        self.other = device(seq, x, y, 1 - core)
        self.peers = [device((seq + k) % NZ, x, y, core) for k in range(1, NZ)]
        self.sends = []

    def slot(self, aa, bb):
        return (1 - self.core) * (aa * 4 + bb) + self.core * (bb * 4 + aa)

    def at(self, aa, bb):
        return (self.seq, self.slot(aa, bb) * 2 + self.core)

    def send(self, src, dst, kind, index, target):
        copy = remote(src, dst, self.sems[kind][0].at[index], self.sems[kind][1].at[index], target)
        copy.start()
        self.sends.append(copy)

    def arrived(self, dst, kind, index):
        remote(dst, dst, self.sems[kind][0].at[index], self.sems[kind][1].at[index], self.other).wait_recv()

    def share(self):
        for j in range(4):
            for k in range(4):
                aa, bb = self.order2[k], self.order1[j]
                p = self.core * (aa * 4 + bb) + (1 - self.core) * (bb * 4 + aa)
                self.send(self.g.at[1 - self.core, p], self.sib.at[p], "s", 4 * j + k, self.other)

    def add(self, j, k):
        p = self.slot(self.order1[k], self.order2[j])
        self.arrived(self.sib.at[p], "s", 4 * j + k)
        self.g[self.core, p] = (self.g[self.core, p].astype(F32) + self.sib[p].astype(F32)).astype(BF16)

    def first(self, j):
        self.add(j, 0)
        far = self.g.at[self.core, self.slot(self.order1[0], self.order2[j])]
        for i, part in enumerate((pl.ds(0, CUT), pl.ds(CUT, CHIP - CUT))):
            self.send(far.at[part], self.p1.at[j, part], "1", 4 * j + i, self.at(self.order1[1 + i], self.b))
        for k in range(1, 4):
            self.add(j, k)

    def middle(self, j):
        for i, part in enumerate((pl.ds(0, CUT), pl.ds(CUT, CHIP - CUT))):
            near = self.g.at[self.core, self.slot(self.order1[1 + i], self.order2[j])]
            self.arrived(self.p1.at[j, part], "1", 4 * j + i)
            near[part] = (near[part].astype(F32) + self.p1[j, part].astype(F32)).astype(BF16)
            self.send(near, self.q1.at[j, i], "1", 4 * j + 2 + i, self.at(self.order1[1 + i], self.b))

    def last(self, j):
        own = self.g.at[self.core, self.slot(self.a, self.order2[j])]
        self.arrived(self.q1.at[j, 0], "1", 4 * j + 2)
        self.arrived(self.q1.at[j, 1], "1", 4 * j + 3)
        own[...] = (own[...].astype(F32) + self.q1[j, 0].astype(F32) + self.q1[j, 1].astype(F32)).astype(BF16)
        parts = (pl.ds(0, CUT), pl.ds(CUT, CHIP - CUT))
        if j == 0:
            for i in range(2):
                self.send(own.at[parts[i]], self.p2.at[parts[i]], "2", i, self.at(self.a, self.order2[1 + i]))
        elif j < 3:
            i = j - 1
            part = parts[i]
            self.arrived(self.p2.at[part], "2", i)
            own[part] = (own[part].astype(F32) + self.p2[part].astype(F32)).astype(BF16)
            self.send(own, self.q2.at[i], "2", 2 + i, self.at(self.a, self.order2[1 + i]))

    def spread(self, total):
        own = self.g.at[self.core, self.slot(self.a, self.b)]
        self.arrived(self.q2.at[0], "2", 2)
        self.arrived(self.q2.at[1], "2", 3)
        total[...] = own[...].astype(F32) + self.q2[0].astype(F32) + self.q2[1].astype(F32)
        for piece in range(8):
            r0, c0 = ROWS[piece // 2], COLS[piece % 2]
            self.pieces[piece] = total[r0 : r0 + 24, c0 : c0 + 384].astype(BF16)
        for k in range(1, NZ):
            target = (self.seq + k) % NZ
            self.send(self.pieces.at[target], self.rz.at[k - 1], "z", k - 1, self.peers[k - 1])

    def finish(self):
        acc = self.pieces[self.seq].astype(F32)
        for k in range(1, NZ):
            self.arrived(self.rz.at[k - 1], "z", k - 1)
            acc = acc + self.rz[k - 1].astype(F32)
        self.zz[self.core, self.seq] = acc.astype(BF16)
        mine = self.zz.at[self.core, self.seq]
        for k in range(1, NZ):
            self.send(mine, mine, "g", k - 1, self.peers[k - 1])
        self.send(mine, mine, "w", 0, self.other)

    def pass_on(self):
        for k in range(1, NZ):
            piece = self.zz.at[self.core, (self.seq + NZ - k) % NZ]
            self.arrived(piece, "g", k - 1)
            self.send(piece, piece, "w", k, self.other)

    def collect(self, gout, first, second):
        for k in range(NZ):
            self.arrived(self.zz.at[1 - self.core, (self.seq + NZ - k) % NZ], "w", k)
        for m, index in enumerate((first, second)):
            for piece in range(8):
                r0, c0 = ROWS[piece // 2], COLS[piece % 2]
                gout[index, r0 : r0 + 24, c0 : c0 + 384] = self.zz[m, piece].astype(F32) * (1.0 / 32.0)
        for copy in self.sends:
            copy.wait_send()


def sublayer_kernel(
    tokwin, cot, w, ask, give, give_col, out, gin, gout,
    wv, tw, ct, qh, kh, vh, dh, oh, gh, kg, vg, dwin, bias, stat, sw, rows, tok_t, cot_t, att, dq, dk, dv, total,
    *rest,
):
    refs = [rest[:9], rest[9:18]]
    ld, sd, rd, st, rt = rest[18:23]
    sems = []
    for wave in range(2):
        flat = rest[23 + 12 * wave : 35 + 12 * wave]
        sems.append({kind: (flat[2 * i], flat[2 * i + 1]) for i, kind in enumerate("s12zgw")})
    seq, x, y, core = place()
    up, down = device((seq + 1) % NZ, x, y, core), device((seq + NZ - 1) % NZ, x, y, core)
    up2, down2 = device((seq + 2) % NZ, x, y, core), device((seq + NZ - 2) % NZ, x, y, core)

    loads = [
        pltpu.make_async_copy(cot, ct, ld.at[0]),
        pltpu.make_async_copy(w.at[3], wv.at[3], ld.at[1]),
        pltpu.make_async_copy(tokwin, tw, ld.at[2]),
        pltpu.make_async_copy(w.at[0], wv.at[0], ld.at[3]),
        pltpu.make_async_copy(w.at[1], wv.at[1], ld.at[4]),
        pltpu.make_async_copy(w.at[2], wv.at[2], ld.at[5]),
    ]
    for load in loads:
        load.start()
    greet(neighbours(seq, x, y, core) + [device((seq + k) % NZ, x, y, core) for k in range(1, NZ)])

    loads[0].wait()
    loads[1].wait()
    dwin[3 * BLK : 5 * BLK, :] = dot(ct[...], wv[3]).astype(BF16)

    def around(first, count):
        return dwin.at[pl.ds(first * BLK, count * BLK)]

    halo = [
        remote(around(4, 1), around(2, 1), sd.at[0], rd.at[0], up),
        remote(around(3, 1), around(5, 1), sd.at[1], rd.at[1], down),
        remote(around(3, 1), around(1, 1), sd.at[2], rd.at[2], up),
        remote(around(4, 1), around(6, 1), sd.at[3], rd.at[3], down),
    ]
    for copy in halo:
        copy.start()
    farther = [
        remote(around(2, 1), around(0, 1), sd.at[4], rd.at[4], up),
        remote(around(5, 1), around(7, 1), sd.at[5], rd.at[5], down),
    ]

    for ref in (qh, kh, vh, dh):
        ref[...] = jnp.zeros_like(ref)
    for load in loads[2:]:
        load.wait()

    def project(step, carry):
        at = pl.ds(pl.multiple_of(step * OWN, OWN), OWN)
        rows_in = tw[at, :]
        for m, ref in enumerate((qh, kh, vh)):
            full = dot(rows_in, wv[m]).astype(BF16)
            for h in range(HEADS):
                ref[h, at, 0:HD] = full[:, h * HD : (h + 1) * HD]
        return carry

    lax.fori_loop(0, 4, project, 0)
    for h in range(HEADS):
        dh[h, 3 * BLK : 5 * BLK, 0:HD] = dwin[3 * BLK : 5 * BLK, h * HD : (h + 1) * HD]
    halo[0].wait_recv()
    farther[0].start()
    halo[1].wait_recv()
    farther[1].start()

    row = lax.broadcasted_iota(jnp.int32, (BLK, WINDOW), 0)
    col = lax.broadcasted_iota(jnp.int32, (BLK, WINDOW), 1)
    for i in range(2):
        line = jnp.broadcast_to(ask[i : i + 1, :], (BLK, WINDOW))
        bias[i * BLK : (i + 1) * BLK, :] = jnp.where(col == row + (3 + i) * BLK, 0.0, line)
    lane = lax.broadcasted_iota(jnp.int32, (OWN, BLK), 1)
    stat[...] = jnp.zeros_like(stat)
    mine = slice(3 * BLK, 5 * BLK)

    def ask_head(h, carry):
        k, v, d = kh[h], vh[h], dh[h, mine, :]
        s = dot_t(qh[h, mine, :], k) * SCALE2 + bias[...]
        top = jnp.max(s, axis=1, keepdims=True)
        e = jnp.exp2(s - top)
        norm = jnp.sum(e, axis=1, keepdims=True)
        p = e * (1.0 / norm)
        o = dot(p.astype(BF16), v).astype(BF16)
        oh[h] = o
        delta = jnp.sum(d.astype(F32) * o.astype(F32), axis=1, keepdims=True)
        ds = (p * (dot_t(d, v) - delta)).astype(BF16)
        gh[h] = (dot(ds, k) * SCALE).astype(BF16)
        lse = top + jnp.log2(norm)
        stat[...] = jnp.where(lane == h, lse, jnp.where(lane == h + HEADS, delta, stat[...]))
        return carry

    lax.fori_loop(0, HEADS, ask_head, 0)

    for i in range(2):
        sw[3 + i] = stat[i * BLK : (i + 1) * BLK, :].T[0 : 2 * HEADS, :]
    stats = [
        remote(sw.at[pl.ds(3, 2)], sw.at[pl.ds(1, 2)], st.at[0], rt.at[0], up),
        remote(sw.at[pl.ds(3, 2)], sw.at[pl.ds(5, 2)], st.at[1], rt.at[1], down),
        remote(sw.at[4], sw.at[0], st.at[2], rt.at[2], up2),
        remote(sw.at[3], sw.at[7], st.at[3], rt.at[3], down2),
    ]
    for copy in stats:
        copy.start()

    early = Wave(refs[0], sems[0], seq, x, y, core)
    late = Wave(refs[1], sems[1], seq, x, y, core)

    def partial(dst, lhs, rhs):
        def part(r, carry):
            at = pl.ds(pl.multiple_of(r * 352, 352), 352)
            full = dot(lhs[at, :], rhs[...])
            for k in range(4):
                dst[4 * r + k] = full[k * CHIP : (k + 1) * CHIP, :].astype(BF16)
            return carry

        lax.fori_loop(0, 4, part, 0)

    for h in range(HEADS):
        att[:, h * HD : (h + 1) * HD] = oh[h, :, 0:HD]
        dq[:, h * HD : (h + 1) * HD] = gh[h, :, 0:HD]
    tok_t[...] = tw[mine, :].T
    cot_t[...] = ct[...].T
    partial(early.g.at[0], tok_t, dq)
    partial(early.g.at[1], cot_t, att)
    early.share()

    for i in range(2):
        line = jnp.broadcast_to(give[i : i + 1, :], (BLK, WINDOW)) + give_col[i * BLK : (i + 1) * BLK, :]
        bias[i * BLK : (i + 1) * BLK, :] = jnp.where(col == row + (3 + i) * BLK, 0.0, line)
    early.first(0)
    early.first(1)
    early.first(2)
    early.first(3)
    halo[2].wait_recv()
    halo[3].wait_recv()
    farther[0].wait_recv()
    farther[1].wait_recv()
    for h in range(HEADS):
        dh[h, 0 : 3 * BLK, 0:HD] = dwin[0 : 3 * BLK, h * HD : (h + 1) * HD]
        dh[h, 5 * BLK : 8 * BLK, 0:HD] = dwin[5 * BLK : 8 * BLK, h * HD : (h + 1) * HD]
    for copy in stats:
        copy.wait_recv()
    for i in range(8):
        rows[:, i * BLK : (i + 1) * BLK] = sw[i]

    def give_head(h, carry):
        q, d = qh[h], dh[h]
        lse = rows[pl.ds(h, 1), :]
        delta = rows[pl.ds(h + HEADS, 1), :]
        s = dot_t(kh[h, mine, :], q) * SCALE2 + bias[...]
        p = jnp.exp2(s - lse)
        ds = (p * (dot_t(vh[h, mine, :], d) - delta)).astype(BF16)
        vg[h] = dot(p.astype(BF16), d).astype(BF16)
        kg[h] = (dot(ds, q) * SCALE).astype(BF16)
        return carry

    early.middle(0)
    lax.fori_loop(0, 2, give_head, 0)
    early.middle(1)
    lax.fori_loop(2, 4, give_head, 0)
    early.middle(2)
    early.middle(3)
    early.last(0)
    lax.fori_loop(4, 6, give_head, 0)
    early.last(1)
    lax.fori_loop(6, 8, give_head, 0)
    for h in range(HEADS):
        dk[:, h * HD : (h + 1) * HD] = kg[h, :, 0:HD]
        dv[:, h * HD : (h + 1) * HD] = vg[h, :, 0:HD]
    partial(late.g.at[0], tok_t, dk)
    partial(late.g.at[1], tok_t, dv)
    late.share()
    early.last(2)
    early.last(3)
    for j in range(4):
        late.first(j)
    early.spread(total)
    late.middle(0)
    out[...] = dot_t(att[...], wv[3]).astype(BF16)
    late.middle(1)
    late.middle(2)
    late.middle(3)
    early.finish()
    late.last(0)
    gin[...] = (dot_t(dq[...], wv[0]) + dot_t(dk[...], wv[1]) + dot_t(dv[...], wv[2])).astype(BF16)
    late.last(1)
    late.last(2)
    late.last(3)
    early.pass_on()
    late.spread(total)
    early.collect(gout, 0, 3)
    late.finish()
    late.pass_on()
    late.collect(gout, 1, 2)
    for copy in halo + farther + stats:
        copy.wait_send()


def sublayer(tokwin, cot, w, ask, give, give_col):
    dma = pltpu.SemaphoreType.DMA
    grid16 = (NX * NY, CHIP, HH)
    heads, heads_own = (HEADS, WINDOW, BLK), (HEADS, OWN, BLK)
    bf = lambda *shape: pltpu.VMEM(shape, BF16)
    scratch = [bf(4, D, HH), bf(WINDOW, D), bf(OWN, D)]
    scratch += [bf(*heads)] * 4 + [bf(*heads_own)] * 4
    scratch += [
        bf(WINDOW, HH),
        pltpu.VMEM((OWN, WINDOW), F32),
        pltpu.VMEM((OWN, BLK), F32),
        pltpu.VMEM((8, 2 * HEADS, BLK), F32),
        pltpu.VMEM((2 * HEADS, WINDOW), F32),
        bf(D, OWN),
        bf(D, OWN),
    ]
    scratch += [bf(OWN, HH)] * 4 + [pltpu.VMEM((CHIP, HH), F32)]
    for wave in range(2):
        scratch += [
            bf(2, *grid16),
            bf(*grid16),
            bf(4, CHIP, HH),
            bf(4, 2, CHIP, HH),
            bf(CHIP, HH),
            bf(2, CHIP, HH),
            bf(8, 24, 384),
            bf(7, 24, 384),
            bf(2, 8, 24, 384),
        ]
    scratch += [dma((6,))] + [dma((6,))] * 2 + [dma((4,))] * 2
    for wave in range(2):
        for count in (16, 16, 4, 7, 7, 8):
            scratch += [dma((count,))] * 2
    return pl.pallas_call(
        sublayer_kernel,
        out_shape=(
            jax.ShapeDtypeStruct((OWN, D), BF16),
            jax.ShapeDtypeStruct((OWN, D), BF16),
            jax.ShapeDtypeStruct((4, CHIP, HH), F32),
        ),
        in_specs=[ANY] * 3 + [VMEM] * 3,
        out_specs=(VMEM,) * 3,
        scratch_shapes=scratch,
        compiler_params=pltpu.CompilerParams(
            collective_id=1, has_side_effects=True, vmem_limit_bytes=62 << 20
        ),
        name="sublayer",
    )(tokwin, cot, w, ask, give, give_col)


def biases(columns, lengths, keep):
    seq = lax.axis_index("seq")
    start = (2 * seq + NBLK - 3) % NBLK
    blocks = (start + jnp.arange(8, dtype=jnp.int32)) % NBLK
    mine = 2 * seq + jnp.arange(2, dtype=jnp.int32)
    cut = jnp.arange(lengths.shape[0], dtype=jnp.int32)
    ends = jnp.sum(jnp.where(cut[None, :] <= cut[:, None], lengths[None, :], 0), axis=1)

    def owner(index):
        return jnp.sum((ends[None, :] <= index[:, None]).astype(jnp.int32), axis=1)

    same = owner(mine)[:, None] == owner(blocks)[None, :]
    twice = jnp.concatenate([columns, columns], axis=0)
    columns_mine = lax.dynamic_slice(columns, (2 * seq, 0), (2, columns.shape[1]))
    columns_win = lax.dynamic_slice(twice, (start, 0), (8, columns.shape[1]))
    ask = same & jnp.any(columns_mine[:, None, :] == blocks[None, :, None], axis=2)
    give = same & jnp.any(columns_win[None, :, :] == mine[:, None, None], axis=2)
    kept = keep.reshape(NBLK, BLK)
    kept_win = lax.dynamic_slice(jnp.concatenate([kept, kept], axis=0), (start, 0), (8, BLK))
    kept_mine = lax.dynamic_slice(kept, (2 * seq, 0), (2, BLK))
    ask_rows = jnp.where(ask[:, :, None] & (kept_win == 1)[None], 0.0, NEG).reshape(2, 8 * BLK)
    give_rows = jnp.broadcast_to(jnp.where(give, 0.0, NEG)[:, :, None], (2, 8, BLK)).reshape(2, 8 * BLK)
    give_cols = jnp.where(kept_mine == 1, 0.0, NEG).reshape(2 * BLK, 1)
    return ask_rows.astype(F32), give_rows.astype(F32), give_cols.astype(F32)


def body(tokens, weights, cotangent, col_list, cut_lengths, keep_mask):
    core = lax.axis_index("dp") % 2
    shard = weights.shape[0]
    halves = jnp.transpose(weights, (1, 0, 2)).reshape(2, 2, shard, HH)
    padded = lax.dynamic_update_slice(jnp.zeros((2, 2, CHIP, HH), BF16), halves, (0, 0, shard * core, 0))
    full, window = gather(padded, tokens[0])
    ask, give, give_col = biases(col_list[0], cut_lengths[0], keep_mask[0])
    result, grad_in, summed = sublayer(window, cotangent[0], full.reshape(4, D, HH), ask, give, give_col)
    mine = lax.dynamic_slice(summed, (0, shard * core, 0), (4, shard, HH))
    return (result[None], grad_in[None], jnp.transpose(mine, (1, 0, 2)))


def solution(mesh):
    placed = (
        P("dp", "seq", None),
        P("dp", None, None),
        P("dp", "seq", None),
        P("dp", None, None),
        P("dp", None),
        P("dp", None),
    )
    return jax.shard_map(
        body,
        mesh=mesh,
        in_specs=placed,
        out_specs=(P("dp", "seq", None), P("dp", "seq", None), P("dp", None, None)),
        check_vma=False,
    )
```

```python
import math

import jax
import jax.numpy as jnp
from jax import lax
from jax.experimental import pallas as pl
from jax.experimental.pallas import tpu as pltpu
from jax.sharding import PartitionSpec as P

HD = 88
HEADS = 8
HH = 704
D = 1408
OWN = 256
WINDOW = 1024
BLK = 128
NBLK = 16
NX = 4
NY = 4
NZ = 8
CHIP = 88
CUT = 48
NEG = -1e30
MESH = pl.DeviceIdType.MESH
F32 = jnp.float32
BF16 = jnp.bfloat16
VMEM = pl.BlockSpec(memory_space=pltpu.VMEM)
HBM = pl.BlockSpec(memory_space=pltpu.HBM)
SMEM = pl.BlockSpec(memory_space=pltpu.SMEM)


def place():
    seq = lax.axis_index("seq")
    dp = lax.axis_index("dp")
    return seq, dp // (2 * NY), (dp // 2) % NY, dp % 2


def device(seq, x, y, core):
    return (seq, (x * NY + y) * 2 + core)


def greet(others):
    barrier = pltpu.get_barrier_semaphore()
    for other in others:
        pl.semaphore_signal(barrier, inc=1, device_id=other, device_id_type=MESH)
    pl.semaphore_wait(barrier, len(others))


def neighbours(seq, x, y, core):
    return [
        device(seq, x, y, 1 - core),
        device(seq, (x + 1) % NX, y, core),
        device(seq, (x + NX - 1) % NX, y, core),
        device(seq, x, (y + 1) % NY, core),
        device(seq, x, (y + NY - 1) % NY, core),
    ]


def remote(src, dst, send, recv, target):
    return pltpu.make_async_remote_copy(
        src_ref=src, dst_ref=dst, send_sem=send, recv_sem=recv, device_id=target, device_id_type=MESH
    )


NT = (((1,), (1,)), ((), ()))
SCALE = 1.0 / math.sqrt(HD)
SCALE2 = SCALE * math.log2(math.e)
ROWS = (0, 24, 48, 64)
COLS = (0, 320)


def dot(lhs, rhs):
    return jnp.dot(lhs, rhs, preferred_element_type=F32)


def dot_t(lhs, rhs):
    return lax.dot_general(lhs, rhs, NT, preferred_element_type=F32)


class Gather:
    def __init__(self, wv, blk, sems, seq, x, y, core):
        self.wv, self.blk, self.sems = wv, blk, sems
        self.seq, self.core = seq, core
        self.a, self.b = (1 - core) * x + core * y, (1 - core) * y + core * x
        a, b = self.a, self.b
        self.order1 = (a, (a + 3) % 4, (a + 1) % 4, (a + 2) % 4)
        self.order2 = (b, (b + 3) % 4, (b + 1) % 4, (b + 2) % 4)
        self.other = device(seq, x, y, 1 - core)
        self.sends = []

    def rows(self, half, aa, bb, core, first=0, count=CHIP):
        p = (1 - core) * (aa * 4 + bb) + core * (bb * 4 + aa)
        return self.wv.at[pl.ds(2 * half, 2), p, pl.ds(first, count)]

    def at(self, aa, bb):
        core = self.core
        return (self.seq, ((1 - core) * (aa * 4 + bb) + core * (bb * 4 + aa)) * 2 + core)

    def send(self, src, dst, kind, index, target):
        copy = remote(src, dst, self.sems[kind][0].at[index], self.sems[kind][1].at[index], target)
        copy.start()
        self.sends.append(copy)

    def arrived(self, dst, kind, index):
        remote(dst, dst, self.sems[kind][0].at[index], self.sems[kind][1].at[index], self.other).wait_recv()

    def mine(self, k, j, first=0, count=CHIP):
        return self.rows(self.core, self.order1[k], self.order2[j], self.core, first, count)

    def second(self, src, k):
        for i in range(2):
            self.send(src, self.mine(k, 0), "2", 4 * k + i, self.at(self.a, self.order2[2 - i]))

    def share(self, src, k, j):
        self.send(src, self.mine(k, j), "s", 4 * j + k, self.other)

    def start(self):
        for i in range(2):
            self.send(self.blk, self.mine(0, 0), "1", i, self.at(self.order1[2 - i], self.b))
        self.second(self.blk, 0)
        self.share(self.blk, 0, 0)

    def near(self, i):
        block = self.mine(1 + i, 0)
        self.arrived(block, "1", i)
        part = self.mine(1 + i, 0, CUT * i, (CUT, CHIP - CUT)[i])
        self.send(part, part, "1", 2 + i, self.at(self.order1[2 - i], self.b))
        self.second(block, 1 + i)
        self.share(block, 1 + i, 0)

    def opposite(self):
        self.arrived(self.mine(3, 0, 0, CUT), "1", 2)
        self.arrived(self.mine(3, 0, CUT, CHIP - CUT), "1", 3)
        self.second(self.mine(3, 0), 3)
        self.share(self.mine(3, 0), 3, 0)

    def near2(self, k):
        for i in range(2):
            block = self.mine(k, 1 + i)
            self.arrived(block, "2", 4 * k + i)
            part = self.mine(k, 1 + i, CUT * i, (CUT, CHIP - CUT)[i])
            self.send(part, part, "2", 4 * k + 2 + i, self.at(self.a, self.order2[2 - i]))
            self.share(block, k, 1 + i)

    def far2(self, k):
        self.arrived(self.mine(k, 3, 0, CUT), "2", 4 * k + 2)
        self.arrived(self.mine(k, 3, CUT, CHIP - CUT), "2", 4 * k + 3)
        self.share(self.mine(k, 3), k, 3)

    def finish(self):
        core = self.core
        for j in range(4):
            for k in range(4):
                block = self.rows(1 - core, self.order2[k], self.order1[j], 1 - core)
                self.arrived(block, "s", 4 * j + k)


class Wave:
    def __init__(self, refs, sems, seq, x, y, core):
        self.g, self.sib, self.p1, self.q1, self.p2, self.q2, self.pieces, self.rz, self.zz = refs
        self.sems = sems
        self.seq, self.core = seq, core
        self.a, self.b = (1 - core) * x + core * y, (1 - core) * y + core * x
        a, b = self.a, self.b
        self.order1 = ((a + 2) % 4, (a + 1) % 4, (a + 3) % 4, a)
        self.order2 = ((b + 2) % 4, (b + 1) % 4, (b + 3) % 4, b)
        self.other = device(seq, x, y, 1 - core)
        self.peers = [device((seq + k) % NZ, x, y, core) for k in range(1, NZ)]
        self.sends = []

    def slot(self, aa, bb):
        return (1 - self.core) * (aa * 4 + bb) + self.core * (bb * 4 + aa)

    def at(self, aa, bb):
        return (self.seq, self.slot(aa, bb) * 2 + self.core)

    def send(self, src, dst, kind, index, target):
        copy = remote(src, dst, self.sems[kind][0].at[index], self.sems[kind][1].at[index], target)
        copy.start()
        self.sends.append(copy)

    def arrived(self, dst, kind, index):
        remote(dst, dst, self.sems[kind][0].at[index], self.sems[kind][1].at[index], self.other).wait_recv()

    def share(self):
        for j in range(4):
            for k in range(4):
                aa, bb = self.order2[k], self.order1[j]
                p = self.core * (aa * 4 + bb) + (1 - self.core) * (bb * 4 + aa)
                self.send(self.g.at[1 - self.core, p], self.sib.at[p], "s", 4 * j + k, self.other)

    def add(self, j, k):
        p = self.slot(self.order1[k], self.order2[j])
        self.arrived(self.sib.at[p], "s", 4 * j + k)
        self.g[self.core, p] = (self.g[self.core, p].astype(F32) + self.sib[p].astype(F32)).astype(BF16)

    def first(self, j):
        self.add(j, 0)
        far = self.g.at[self.core, self.slot(self.order1[0], self.order2[j])]
        for i, part in enumerate((pl.ds(0, CUT), pl.ds(CUT, CHIP - CUT))):
            self.send(far.at[part], self.p1.at[j, part], "1", 4 * j + i, self.at(self.order1[1 + i], self.b))
        for k in range(1, 4):
            self.add(j, k)

    def middle(self, j):
        for i, part in enumerate((pl.ds(0, CUT), pl.ds(CUT, CHIP - CUT))):
            near = self.g.at[self.core, self.slot(self.order1[1 + i], self.order2[j])]
            self.arrived(self.p1.at[j, part], "1", 4 * j + i)
            near[part] = (near[part].astype(F32) + self.p1[j, part].astype(F32)).astype(BF16)
            self.send(near, self.q1.at[j, i], "1", 4 * j + 2 + i, self.at(self.order1[1 + i], self.b))

    def last(self, j):
        own = self.g.at[self.core, self.slot(self.a, self.order2[j])]
        self.arrived(self.q1.at[j, 0], "1", 4 * j + 2)
        self.arrived(self.q1.at[j, 1], "1", 4 * j + 3)
        own[...] = (own[...].astype(F32) + self.q1[j, 0].astype(F32) + self.q1[j, 1].astype(F32)).astype(BF16)
        parts = (pl.ds(0, CUT), pl.ds(CUT, CHIP - CUT))
        if j == 0:
            for i in range(2):
                self.send(own.at[parts[i]], self.p2.at[parts[i]], "2", i, self.at(self.a, self.order2[1 + i]))
        elif j < 3:
            i = j - 1
            part = parts[i]
            self.arrived(self.p2.at[part], "2", i)
            own[part] = (own[part].astype(F32) + self.p2[part].astype(F32)).astype(BF16)
            self.send(own, self.q2.at[i], "2", 2 + i, self.at(self.a, self.order2[1 + i]))

    def spread(self, total):
        own = self.g.at[self.core, self.slot(self.a, self.b)]
        self.arrived(self.q2.at[0], "2", 2)
        self.arrived(self.q2.at[1], "2", 3)
        total[...] = own[...].astype(F32) + self.q2[0].astype(F32) + self.q2[1].astype(F32)
        for piece in range(8):
            r0, c0 = ROWS[piece // 2], COLS[piece % 2]
            self.pieces[piece] = total[r0 : r0 + 24, c0 : c0 + 384].astype(BF16)
        for k in range(1, NZ):
            target = (self.seq + k) % NZ
            self.send(self.pieces.at[target], self.rz.at[k - 1], "z", k - 1, self.peers[k - 1])

    def finish(self):
        acc = self.pieces[self.seq].astype(F32)
        for k in range(1, NZ):
            self.arrived(self.rz.at[k - 1], "z", k - 1)
            acc = acc + self.rz[k - 1].astype(F32)
        self.zz[self.core, self.seq] = acc.astype(BF16)
        mine = self.zz.at[self.core, self.seq]
        for k in range(1, NZ):
            self.send(mine, mine, "g", k - 1, self.peers[k - 1])
        self.send(mine, mine, "w", 0, self.other)

    def pass_on(self):
        for k in range(1, NZ):
            piece = self.zz.at[self.core, (self.seq + NZ - k) % NZ]
            self.arrived(piece, "g", k - 1)
            self.send(piece, piece, "w", k, self.other)

    def collect(self, gout, first, second):
        for k in range(NZ):
            self.arrived(self.zz.at[1 - self.core, (self.seq + NZ - k) % NZ], "w", k)
        for m, index in enumerate((first, second)):
            for piece in range(8):
                r0, c0 = ROWS[piece // 2], COLS[piece % 2]
                gout[index, r0 : r0 + 24, c0 : c0 + 384] = self.zz[m, piece].astype(F32) * (1.0 / 32.0)
        for copy in self.sends:
            copy.wait_send()


def sublayer_kernel(
    wsh, tok, cot, cols, cuts, keep, out, gin, gout,
    wv, tw, ct, qh, kh, vh, dh, oh, gh, kg, vg, dwin, bias, bias2, stat, sw, rows, tok_t, cot_t, att, dq, dk, dv,
    total, sib, blk,
    *rest,
):
    refs = [rest[:9], rest[9:18]]
    ld, sd, rd, st, rt = rest[18:23]
    sems = []
    for wave in range(2):
        flat = rest[23 + 12 * wave : 35 + 12 * wave]
        sems.append({kind: (flat[2 * i], flat[2 * i + 1]) for i, kind in enumerate("s12zgw")})
    flat = rest[47:]
    gather_sems = {kind: (flat[2 * i], flat[2 * i + 1]) for i, kind in enumerate("xt12s")}
    seq, x, y, core = place()
    other = device(seq, x, y, 1 - core)
    up, down = device((seq + 1) % NZ, x, y, core), device((seq + NZ - 1) % NZ, x, y, core)
    up2, down2 = device((seq + 2) % NZ, x, y, core), device((seq + NZ - 2) % NZ, x, y, core)

    def halo_rows(first, count):
        return tw.at[pl.ds(first * BLK, count * BLK)]

    load_cot = pltpu.make_async_copy(cot, ct, ld.at[0])
    load_tok = pltpu.make_async_copy(tok, halo_rows(3, 2), ld.at[1])
    load_cot.start()
    load_tok.start()
    greet(neighbours(seq, x, y, core) + [device((seq + k) % NZ, x, y, core) for k in range(1, NZ)])

    swap = remote(
        wsh.at[pl.ds(2 * (1 - core), 2)], sib, gather_sems["x"][0].at[0], gather_sems["x"][1].at[0], other
    )
    swap.start()
    low, high = tok.at[pl.ds(0, BLK)], tok.at[pl.ds(BLK, BLK)]
    tsend, trecv = gather_sems["t"]
    edges = [
        remote(high, halo_rows(2, 1), tsend.at[0], trecv.at[0], up),
        remote(low, halo_rows(5, 1), tsend.at[1], trecv.at[1], down),
        remote(low, halo_rows(1, 1), tsend.at[2], trecv.at[2], up),
        remote(high, halo_rows(6, 1), tsend.at[3], trecv.at[3], down),
    ]
    for copy in edges:
        copy.start()
    edges += [
        remote(halo_rows(2, 1), halo_rows(0, 1), tsend.at[4], trecv.at[4], up),
        remote(halo_rows(5, 1), halo_rows(7, 1), tsend.at[5], trecv.at[5], down),
    ]
    swap.wait_recv()
    ours = wsh[pl.ds(2 * core, 2)]
    theirs = sib[...]
    shard = ours.shape[1]
    blk[:, 0:shard, :] = jnp.where(core == 0, ours, theirs)
    blk[:, shard:CHIP, :] = jnp.where(core == 0, theirs, ours)
    weights = Gather(wv, blk, gather_sems, seq, x, y, core)
    own_rows = pltpu.make_async_copy(blk, weights.mine(0, 0), ld.at[2])
    own_rows.start()
    weights.start()

    blocks = [(2 * seq + NBLK - 3 + i) % NBLK for i in range(8)]
    ends = []
    for c in range(5):
        ends.append(cuts[c] if c == 0 else ends[-1] + cuts[c])

    def owner(index):
        return sum([jnp.where(end <= index, 1, 0) for end in ends])

    owners = [owner(e) for e in blocks]
    row = lax.broadcasted_iota(jnp.int32, (BLK, BLK), 0)
    col = lax.broadcasted_iota(jnp.int32, (BLK, BLK), 1)

    def listed(asks, key):
        found = jnp.where(cols[asks, 0] == key, 1, 0)
        for n in range(1, 5):
            found = found + jnp.where(cols[asks, n] == key, 1, 0)
        return found

    def test(asks, key, same):
        return jnp.where((listed(asks, key) > 0) & same, 0.0, NEG)

    for i in range(2):
        at = slice(i * BLK, (i + 1) * BLK)
        own_keep = jnp.where(keep[pl.ds(blocks[3 + i], 1), :] == 1, 0.0, NEG)
        own_keep = jnp.broadcast_to(own_keep, (BLK, BLK)).T
        for e in range(8):
            same = owners[e] == owners[3 + i]
            line = jnp.where(keep[pl.ds(blocks[e], 1), :] == 1, 0.0, NEG)
            tile = jnp.broadcast_to(line + test(blocks[3 + i], blocks[e], same), (BLK, BLK))
            back = own_keep + test(blocks[e], blocks[3 + i], same)
            if e == 3 + i:
                tile = jnp.where(row == col, 0.0, tile)
                back = jnp.where(row == col, 0.0, back)
            bias[at, e * BLK : (e + 1) * BLK] = tile
            bias2[at, e * BLK : (e + 1) * BLK] = back
    weights.near(0)
    weights.near(1)
    for ref in (qh, kh, vh, dh):
        ref[...] = jnp.zeros_like(ref)
    weights.opposite()
    weights.near2(0)
    weights.near2(1)
    load_cot.wait()
    load_tok.wait()
    weights.near2(2)
    edges[0].wait_recv()
    edges[4].start()
    edges[1].wait_recv()
    edges[5].start()
    weights.near2(3)
    mine = slice(3 * BLK, 5 * BLK)
    tok_t[...] = tw[mine, :].T
    cot_t[...] = ct[...].T
    for k in range(4):
        weights.far2(k)
    weights.finish()
    own_rows.wait()

    dwin[3 * BLK : 5 * BLK, :] = dot(ct[...], wv[3].reshape(D, HH)).astype(BF16)

    def around(first, count):
        return dwin.at[pl.ds(first * BLK, count * BLK)]

    halo = [
        remote(around(4, 1), around(2, 1), sd.at[0], rd.at[0], up),
        remote(around(3, 1), around(5, 1), sd.at[1], rd.at[1], down),
        remote(around(3, 1), around(1, 1), sd.at[2], rd.at[2], up),
        remote(around(4, 1), around(6, 1), sd.at[3], rd.at[3], down),
    ]
    for copy in halo:
        copy.start()
    farther = [
        remote(around(2, 1), around(0, 1), sd.at[4], rd.at[4], up),
        remote(around(5, 1), around(7, 1), sd.at[5], rd.at[5], down),
    ]
    for copy in edges[2:]:
        copy.wait_recv()

    def project(step, carry):
        at = pl.ds(pl.multiple_of(step * OWN, OWN), OWN)
        rows_in = tw[at, :]
        for m, ref in enumerate((qh, kh, vh)):
            full = dot(rows_in, wv[m].reshape(D, HH)).astype(BF16)
            for h in range(HEADS):
                ref[h, at, 0:HD] = full[:, h * HD : (h + 1) * HD]
        return carry

    lax.fori_loop(0, 4, project, 0)
    for h in range(HEADS):
        dh[h, 3 * BLK : 5 * BLK, 0:HD] = dwin[3 * BLK : 5 * BLK, h * HD : (h + 1) * HD]
    halo[0].wait_recv()
    farther[0].start()
    halo[1].wait_recv()
    farther[1].start()

    lane = lax.broadcasted_iota(jnp.int32, (OWN, BLK), 1)
    stat[...] = jnp.zeros_like(stat)

    def ask_head(h, carry):
        k, v, d = kh[h], vh[h], dh[h, mine, :]
        s = dot_t(qh[h, mine, :], k) * SCALE2 + bias[...]
        top = jnp.max(s, axis=1, keepdims=True)
        e = jnp.exp2(s - top)
        norm = jnp.sum(e, axis=1, keepdims=True)
        p = e * (1.0 / norm)
        o = dot(p.astype(BF16), v).astype(BF16)
        oh[h] = o
        delta = jnp.sum(d.astype(F32) * o.astype(F32), axis=1, keepdims=True)
        ds = (p * (dot_t(d, v) - delta)).astype(BF16)
        gh[h] = (dot(ds, k) * SCALE).astype(BF16)
        lse = top + jnp.log2(norm)
        stat[...] = jnp.where(lane == h, lse, jnp.where(lane == h + HEADS, delta, stat[...]))
        return carry

    lax.fori_loop(0, HEADS, ask_head, 0)

    for i in range(2):
        sw[3 + i] = stat[i * BLK : (i + 1) * BLK, :].T[0 : 2 * HEADS, :]
    stats = [
        remote(sw.at[pl.ds(3, 2)], sw.at[pl.ds(1, 2)], st.at[0], rt.at[0], up),
        remote(sw.at[pl.ds(3, 2)], sw.at[pl.ds(5, 2)], st.at[1], rt.at[1], down),
        remote(sw.at[4], sw.at[0], st.at[2], rt.at[2], up2),
        remote(sw.at[3], sw.at[7], st.at[3], rt.at[3], down2),
    ]
    for copy in stats:
        copy.start()

    early = Wave(refs[0], sems[0], seq, x, y, core)
    late = Wave(refs[1], sems[1], seq, x, y, core)

    def partial(dst, lhs, rhs):
        def part(r, carry):
            at = pl.ds(pl.multiple_of(r * 352, 352), 352)
            full = dot(lhs[at, :], rhs[...])
            for k in range(4):
                dst[4 * r + k] = full[k * CHIP : (k + 1) * CHIP, :].astype(BF16)
            return carry

        lax.fori_loop(0, 4, part, 0)

    for h in range(HEADS):
        att[:, h * HD : (h + 1) * HD] = oh[h, :, 0:HD]
        dq[:, h * HD : (h + 1) * HD] = gh[h, :, 0:HD]
    partial(early.g.at[0], tok_t, dq)
    partial(early.g.at[1], cot_t, att)
    early.share()

    early.first(0)
    early.first(1)
    early.first(2)
    early.first(3)
    halo[2].wait_recv()
    halo[3].wait_recv()
    farther[0].wait_recv()
    farther[1].wait_recv()
    for h in range(HEADS):
        dh[h, 0 : 3 * BLK, 0:HD] = dwin[0 : 3 * BLK, h * HD : (h + 1) * HD]
        dh[h, 5 * BLK : 8 * BLK, 0:HD] = dwin[5 * BLK : 8 * BLK, h * HD : (h + 1) * HD]
    for copy in stats:
        copy.wait_recv()
    for i in range(8):
        rows[:, i * BLK : (i + 1) * BLK] = sw[i]

    def give_head(h, carry):
        q, d = qh[h], dh[h]
        lse = rows[pl.ds(h, 1), :]
        delta = rows[pl.ds(h + HEADS, 1), :]
        s = dot_t(kh[h, mine, :], q) * SCALE2 + bias2[...]
        p = jnp.exp2(s - lse)
        ds = (p * (dot_t(vh[h, mine, :], d) - delta)).astype(BF16)
        vg[h] = dot(p.astype(BF16), d).astype(BF16)
        kg[h] = (dot(ds, q) * SCALE).astype(BF16)
        return carry

    early.middle(0)
    lax.fori_loop(0, 2, give_head, 0)
    early.middle(1)
    lax.fori_loop(2, 4, give_head, 0)
    early.middle(2)
    early.middle(3)
    early.last(0)
    lax.fori_loop(4, 6, give_head, 0)
    early.last(1)
    lax.fori_loop(6, 8, give_head, 0)
    for h in range(HEADS):
        dk[:, h * HD : (h + 1) * HD] = kg[h, :, 0:HD]
        dv[:, h * HD : (h + 1) * HD] = vg[h, :, 0:HD]
    partial(late.g.at[0], tok_t, dk)
    partial(late.g.at[1], tok_t, dv)
    late.share()
    early.last(2)
    early.last(3)
    for j in range(4):
        late.first(j)
    early.spread(total)
    late.middle(0)
    out[...] = dot_t(att[...], wv[3].reshape(D, HH)).astype(BF16)
    late.middle(1)
    late.middle(2)
    late.middle(3)
    early.finish()
    late.last(0)
    gin[...] = (dot_t(dq[...], wv[0].reshape(D, HH)) + dot_t(dk[...], wv[1].reshape(D, HH)) + dot_t(dv[...], wv[2].reshape(D, HH))).astype(BF16)
    late.last(1)
    late.last(2)
    late.last(3)
    early.pass_on()
    late.spread(total)
    early.collect(gout, 0, 3)
    late.finish()
    late.pass_on()
    late.collect(gout, 1, 2)
    for copy in halo + farther + stats + edges + weights.sends + [swap]:
        copy.wait_send()


def sublayer(wsh, tok, cot, cols, cuts, keep):
    dma = pltpu.SemaphoreType.DMA
    grid16 = (NX * NY, CHIP, HH)
    heads, heads_own = (HEADS, WINDOW, BLK), (HEADS, OWN, BLK)
    bf = lambda *shape: pltpu.VMEM(shape, BF16)
    scratch = [bf(4, *grid16), bf(WINDOW, D), bf(OWN, D)]
    scratch += [bf(*heads)] * 4 + [bf(*heads_own)] * 4
    scratch += [
        bf(WINDOW, HH),
        pltpu.VMEM((OWN, WINDOW), F32),
        pltpu.VMEM((OWN, WINDOW), F32),
        pltpu.VMEM((OWN, BLK), F32),
        pltpu.VMEM((8, 2 * HEADS, BLK), F32),
        pltpu.VMEM((2 * HEADS, WINDOW), F32),
        bf(D, OWN),
        bf(D, OWN),
    ]
    scratch += [bf(OWN, HH)] * 4 + [pltpu.VMEM((CHIP, HH), F32)]
    scratch += [bf(2, wsh.shape[1], HH), bf(2, CHIP, HH)]
    for wave in range(2):
        scratch += [
            bf(2, *grid16),
            bf(*grid16),
            bf(4, CHIP, HH),
            bf(4, 2, CHIP, HH),
            bf(CHIP, HH),
            bf(2, CHIP, HH),
            bf(8, 24, 384),
            bf(7, 24, 384),
            bf(2, 8, 24, 384),
        ]
    scratch += [dma((3,))] + [dma((6,))] * 2 + [dma((4,))] * 2
    for wave in range(2):
        for count in (16, 16, 4, 7, 7, 8):
            scratch += [dma((count,))] * 2
    for count in (1, 6, 4, 16, 16):
        scratch += [dma((count,))] * 2
    return pl.pallas_call(
        sublayer_kernel,
        out_shape=(
            jax.ShapeDtypeStruct((OWN, D), BF16),
            jax.ShapeDtypeStruct((OWN, D), BF16),
            jax.ShapeDtypeStruct((4, CHIP, HH), F32),
        ),
        in_specs=[VMEM, HBM, HBM, SMEM, SMEM, VMEM],
        out_specs=(VMEM,) * 3,
        scratch_shapes=scratch,
        compiler_params=pltpu.CompilerParams(
            collective_id=1, has_side_effects=True, vmem_limit_bytes=62 << 20
        ),
        name="sublayer",
    )(wsh, tok, cot, cols, cuts, keep)


def body(tokens, weights, cotangent, col_list, cut_lengths, keep_mask):
    core = lax.axis_index("dp") % 2
    shard = weights.shape[0]
    result, grad_in, summed = sublayer(
        jnp.transpose(weights, (1, 0, 2)),
        tokens[0],
        cotangent[0],
        col_list[0],
        cut_lengths[0],
        keep_mask[0].reshape(NBLK, BLK),
    )
    mine = lax.dynamic_slice(summed, (0, shard * core, 0), (4, shard, HH))
    return (result[None], grad_in[None], jnp.transpose(mine, (1, 0, 2)))


def solution(mesh):
    placed = (
        P("dp", "seq", None),
        P("dp", None, None),
        P("dp", "seq", None),
        P("dp", None, None),
        P("dp", None),
        P("dp", None),
    )
    return jax.shard_map(
        body,
        mesh=mesh,
        in_specs=placed,
        out_specs=(P("dp", "seq", None), P("dp", "seq", None), P("dp", None, None)),
        check_vma=False,
    )
```

```python
import math

import jax
import jax.numpy as jnp
from jax import lax
from jax.experimental import pallas as pl
from jax.experimental.pallas import tpu as pltpu
from jax.sharding import PartitionSpec as P

HD = 88
HEADS = 8
HH = 704
D = 1408
OWN = 256
WINDOW = 1024
BLK = 128
NBLK = 16
NX = 4
NY = 4
NZ = 8
CHIP = 88
CUT = 48
NEG = -1e30
MESH = pl.DeviceIdType.MESH
F32 = jnp.float32
BF16 = jnp.bfloat16
VMEM = pl.BlockSpec(memory_space=pltpu.VMEM)
HBM = pl.BlockSpec(memory_space=pltpu.HBM)
SMEM = pl.BlockSpec(memory_space=pltpu.SMEM)


def place():
    seq = lax.axis_index("seq")
    dp = lax.axis_index("dp")
    return seq, dp // (2 * NY), (dp // 2) % NY, dp % 2


def device(seq, x, y, core):
    return (seq, (x * NY + y) * 2 + core)


def greet(others):
    barrier = pltpu.get_barrier_semaphore()
    for other in others:
        pl.semaphore_signal(barrier, inc=1, device_id=other, device_id_type=MESH)
    pl.semaphore_wait(barrier, len(others))


def neighbours(seq, x, y, core):
    return [
        device(seq, x, y, 1 - core),
        device(seq, (x + 1) % NX, y, core),
        device(seq, (x + NX - 1) % NX, y, core),
        device(seq, x, (y + 1) % NY, core),
        device(seq, x, (y + NY - 1) % NY, core),
        device(seq, (x + 2) % NX, y, core),
        device(seq, x, (y + 2) % NY, core),
    ]


def remote(src, dst, send, recv, target):
    return pltpu.make_async_remote_copy(
        src_ref=src, dst_ref=dst, send_sem=send, recv_sem=recv, device_id=target, device_id_type=MESH
    )


NT = (((1,), (1,)), ((), ()))
SCALE = 1.0 / math.sqrt(HD)
SCALE2 = SCALE * math.log2(math.e)
ROWS = (0, 24, 48, 64)
COLS = (0, 320)


def dot(lhs, rhs):
    return jnp.dot(lhs, rhs, preferred_element_type=F32)


def dot_t(lhs, rhs):
    return lax.dot_general(lhs, rhs, NT, preferred_element_type=F32)


class Gather:
    def __init__(self, wv, blk, sems, seq, x, y, core):
        self.wv, self.blk, self.sems = wv, blk, sems
        self.seq, self.core = seq, core
        self.a, self.b = (1 - core) * x + core * y, (1 - core) * y + core * x
        a, b = self.a, self.b
        self.order1 = (a, (a + 3) % 4, (a + 1) % 4, (a + 2) % 4)
        self.order2 = (b, (b + 3) % 4, (b + 1) % 4, (b + 2) % 4)
        self.other = device(seq, x, y, 1 - core)
        self.sends = []

    def rows(self, half, m, aa, bb, core, first=0, count=CHIP):
        p = (1 - core) * (aa * 4 + bb) + core * (bb * 4 + aa)
        return self.wv.at[2 * half + m, p, pl.ds(first, count)]

    def at(self, aa, bb):
        core = self.core
        return (self.seq, ((1 - core) * (aa * 4 + bb) + core * (bb * 4 + aa)) * 2 + core)

    def send(self, src, dst, kind, index, target):
        copy = remote(src, dst, self.sems[kind][0].at[index], self.sems[kind][1].at[index], target)
        copy.start()
        self.sends.append(copy)

    def arrived(self, dst, kind, index):
        remote(dst, dst, self.sems[kind][0].at[index], self.sems[kind][1].at[index], self.other).wait_recv()

    def mine(self, m, k, j, first=0, count=CHIP):
        return self.rows(self.core, m, self.order1[k], self.order2[j], self.core, first, count)

    def second(self, src, m, k):
        for i in range(2):
            self.send(src, self.mine(m, k, 0), "2", 16 * m + 4 * k + i, self.at(self.a, self.order2[2 - i]))

    def share(self, src, m, k, j):
        self.send(src, self.mine(m, k, j), "s", 16 * m + 4 * j + k, self.other)

    def start(self, m):
        src = self.blk.at[m]
        for i in range(2):
            self.send(src, self.mine(m, 0, 0), "1", 4 * m + i, self.at(self.order1[2 - i], self.b))
        self.second(src, m, 0)
        self.share(src, m, 0, 0)

    def near(self, m, i):
        block = self.mine(m, 1 + i, 0)
        self.arrived(block, "1", 4 * m + i)
        part = self.mine(m, 1 + i, 0, CUT * i, (CUT, CHIP - CUT)[i])
        self.send(part, part, "1", 4 * m + 2 + i, self.at(self.order1[2 - i], self.b))
        self.second(block, m, 1 + i)
        self.share(block, m, 1 + i, 0)

    def opposite(self, m):
        self.arrived(self.mine(m, 3, 0, 0, CUT), "1", 4 * m + 2)
        self.arrived(self.mine(m, 3, 0, CUT, CHIP - CUT), "1", 4 * m + 3)
        self.second(self.mine(m, 3, 0), m, 3)
        self.share(self.mine(m, 3, 0), m, 3, 0)

    def near2(self, m, k):
        for i in range(2):
            block = self.mine(m, k, 1 + i)
            self.arrived(block, "2", 16 * m + 4 * k + i)
            part = self.mine(m, k, 1 + i, CUT * i, (CUT, CHIP - CUT)[i])
            self.send(part, part, "2", 16 * m + 4 * k + 2 + i, self.at(self.a, self.order2[2 - i]))
            self.share(block, m, k, 1 + i)

    def far2(self, m, k):
        self.arrived(self.mine(m, k, 3, 0, CUT), "2", 16 * m + 4 * k + 2)
        self.arrived(self.mine(m, k, 3, CUT, CHIP - CUT), "2", 16 * m + 4 * k + 3)
        self.share(self.mine(m, k, 3), m, k, 3)

    def finish(self):
        core = self.core
        for m in range(2):
            for j in range(4):
                for k in range(4):
                    block = self.rows(1 - core, m, self.order2[k], self.order1[j], 1 - core)
                    self.arrived(block, "s", 16 * m + 4 * j + k)


class Wave:
    def __init__(self, refs, sems, seq, x, y, core):
        self.g, self.sib, self.p1, self.q1, self.q2, self.pieces, self.rz, self.zz = refs
        self.sems = sems
        self.seq, self.core = seq, core
        self.a, self.b = (1 - core) * x + core * y, (1 - core) * y + core * x
        a, b = self.a, self.b
        self.order1 = ((a + 2) % 4, (a + 1) % 4, (a + 3) % 4, a)
        self.order2 = ((b + 2) % 4, (b + 1) % 4, (b + 3) % 4, b)
        self.other = device(seq, x, y, 1 - core)
        self.peers = [device((seq + k) % NZ, x, y, core) for k in range(1, NZ)]
        self.sends = []

    def slot(self, aa, bb):
        return (1 - self.core) * (aa * 4 + bb) + self.core * (bb * 4 + aa)

    def at(self, aa, bb):
        return (self.seq, self.slot(aa, bb) * 2 + self.core)

    def send(self, src, dst, kind, index, target):
        copy = remote(src, dst, self.sems[kind][0].at[index], self.sems[kind][1].at[index], target)
        copy.start()
        self.sends.append(copy)

    def arrived(self, dst, kind, index):
        remote(dst, dst, self.sems[kind][0].at[index], self.sems[kind][1].at[index], self.other).wait_recv()

    def share(self):
        for j in range(4):
            for k in range(4):
                aa, bb = self.order2[k], self.order1[j]
                p = self.core * (aa * 4 + bb) + (1 - self.core) * (bb * 4 + aa)
                self.send(self.g.at[1 - self.core, p], self.sib.at[p], "s", 4 * j + k, self.other)

    def add(self, j, k):
        p = self.slot(self.order1[k], self.order2[j])
        self.arrived(self.sib.at[p], "s", 4 * j + k)
        self.g[self.core, p] = (self.g[self.core, p].astype(F32) + self.sib[p].astype(F32)).astype(BF16)

    def first(self, j):
        self.add(j, 0)
        far = self.g.at[self.core, self.slot(self.order1[0], self.order2[j])]
        for i, part in enumerate((pl.ds(0, CUT), pl.ds(CUT, CHIP - CUT))):
            self.send(far.at[part], self.p1.at[j, part], "1", 4 * j + i, self.at(self.order1[1 + i], self.b))
        for k in range(1, 4):
            self.add(j, k)

    def middle(self, j):
        for i, part in enumerate((pl.ds(0, CUT), pl.ds(CUT, CHIP - CUT))):
            near = self.g.at[self.core, self.slot(self.order1[1 + i], self.order2[j])]
            self.arrived(self.p1.at[j, part], "1", 4 * j + i)
            near[part] = (near[part].astype(F32) + self.p1[j, part].astype(F32)).astype(BF16)
            self.send(near, self.q1.at[j, i], "1", 4 * j + 2 + i, self.at(self.order1[1 + i], self.b))

    def last(self, j):
        own = self.g.at[self.core, self.slot(self.a, self.order2[j])]
        self.arrived(self.q1.at[j, 0], "1", 4 * j + 2)
        self.arrived(self.q1.at[j, 1], "1", 4 * j + 3)
        own[...] = (own[...].astype(F32) + self.q1[j, 0].astype(F32) + self.q1[j, 1].astype(F32)).astype(BF16)
        if j < 3:
            self.send(own, self.q2.at[j], "2", j, self.at(self.a, self.order2[j]))

    def spread(self, total):
        acc = self.g[self.core, self.slot(self.a, self.b)].astype(F32)
        for k in range(3):
            self.arrived(self.q2.at[k], "2", k)
            acc = acc + self.q2[k].astype(F32)
        total[...] = acc
        for piece in range(8):
            r0, c0 = ROWS[piece // 2], COLS[piece % 2]
            self.pieces[piece] = total[r0 : r0 + 24, c0 : c0 + 384].astype(BF16)
        for k in range(1, NZ):
            target = (self.seq + k) % NZ
            self.send(self.pieces.at[target], self.rz.at[k - 1], "z", k - 1, self.peers[k - 1])

    def finish(self):
        acc = self.pieces[self.seq].astype(F32)
        for k in range(1, NZ):
            self.arrived(self.rz.at[k - 1], "z", k - 1)
            acc = acc + self.rz[k - 1].astype(F32)
        self.zz[self.core, self.seq] = acc.astype(BF16)
        mine = self.zz.at[self.core, self.seq]
        for k in range(1, NZ):
            self.send(mine, mine, "g", k - 1, self.peers[k - 1])
        self.send(mine, mine, "w", 0, self.other)

    def pass_on(self):
        for k in range(1, NZ):
            piece = self.zz.at[self.core, (self.seq + NZ - k) % NZ]
            self.arrived(piece, "g", k - 1)
            self.send(piece, piece, "w", k, self.other)

    def collect(self, gout, first, second):
        for k in range(NZ):
            self.arrived(self.zz.at[1 - self.core, (self.seq + NZ - k) % NZ], "w", k)
        for m, index in enumerate((first, second)):
            for piece in range(8):
                r0, c0 = ROWS[piece // 2], COLS[piece % 2]
                gout[index, r0 : r0 + 24, c0 : c0 + 384] = self.zz[m, piece].astype(F32) * (1.0 / 32.0)
        for copy in self.sends:
            copy.wait_send()


def sublayer_kernel(
    wsh, tok, cot, cols, cuts, keep, out, gin, gout,
    wv, tw, ct, qh, kh, vh, dh, oh, gh, kg, vg, dwin, bias, bias2, stat, sw, rows, tok_t, cot_t, att, dq, dk, dv,
    total, sib, blk,
    *rest,
):
    refs = [rest[:8], rest[8:16]]
    ld, sd, rd, st, rt = rest[16:21]
    sems = []
    for wave in range(2):
        flat = rest[21 + 12 * wave : 33 + 12 * wave]
        sems.append({kind: (flat[2 * i], flat[2 * i + 1]) for i, kind in enumerate("s12zgw")})
    flat = rest[45:]
    gather_sems = {kind: (flat[2 * i], flat[2 * i + 1]) for i, kind in enumerate("xt12s")}
    seq, x, y, core = place()
    other = device(seq, x, y, 1 - core)
    up, down = device((seq + 1) % NZ, x, y, core), device((seq + NZ - 1) % NZ, x, y, core)
    up2, down2 = device((seq + 2) % NZ, x, y, core), device((seq + NZ - 2) % NZ, x, y, core)

    def halo_rows(first, count):
        return tw.at[pl.ds(first * BLK, count * BLK)]

    load_cot = pltpu.make_async_copy(cot, ct, ld.at[0])
    load_tok = pltpu.make_async_copy(tok, halo_rows(3, 2), ld.at[1])
    load_cot.start()
    load_tok.start()
    greet(neighbours(seq, x, y, core) + [device((seq + k) % NZ, x, y, core) for k in range(1, NZ)])

    swaps = []
    for m in range(2):
        xsend, xrecv = gather_sems["x"]
        swaps.append(remote(wsh.at[2 * (1 - core) + m], sib.at[m], xsend.at[m], xrecv.at[m], other))
        swaps[m].start()
    low, high = tok.at[pl.ds(0, BLK)], tok.at[pl.ds(BLK, BLK)]
    tsend, trecv = gather_sems["t"]
    edges = [
        remote(high, halo_rows(2, 1), tsend.at[0], trecv.at[0], up),
        remote(low, halo_rows(5, 1), tsend.at[1], trecv.at[1], down),
        remote(low, halo_rows(1, 1), tsend.at[2], trecv.at[2], up),
        remote(high, halo_rows(6, 1), tsend.at[3], trecv.at[3], down),
    ]
    for copy in edges:
        copy.start()
    edges += [
        remote(halo_rows(2, 1), halo_rows(0, 1), tsend.at[4], trecv.at[4], up),
        remote(halo_rows(5, 1), halo_rows(7, 1), tsend.at[5], trecv.at[5], down),
    ]
    weights = Gather(wv, blk, gather_sems, seq, x, y, core)
    own_rows = []
    for m in range(2):
        swaps[m].wait_recv()
        ours = wsh[2 * core + m]
        theirs = sib[m]
        shard = ours.shape[0]
        blk[m, 0:shard, :] = jnp.where(core == 0, ours, theirs)
        blk[m, shard:CHIP, :] = jnp.where(core == 0, theirs, ours)
        own_rows.append(pltpu.make_async_copy(blk.at[m], weights.mine(m, 0, 0), ld.at[2 + m]))
        own_rows[m].start()
        weights.start(m)

    for m in range(2):
        weights.near(m, 0)
        weights.near(m, 1)
        weights.near2(m, 0)
    for m in range(2):
        weights.opposite(m)
    weights.near2(0, 1)
    weights.near2(1, 1)
    weights.far2(0, 0)
    weights.near2(0, 2)
    weights.far2(1, 0)
    weights.near2(1, 2)
    edges[0].wait_recv()
    edges[4].start()
    edges[1].wait_recv()
    edges[5].start()
    weights.near2(0, 3)
    weights.near2(1, 3)
    load_cot.wait()
    load_tok.wait()
    blocks = [(2 * seq + NBLK - 3 + i) % NBLK for i in range(8)]
    ends = []
    for c in range(5):
        ends.append(cuts[c] if c == 0 else ends[-1] + cuts[c])

    def owner(index):
        return sum([jnp.where(end <= index, 1, 0) for end in ends])

    owners = [owner(e) for e in blocks]
    row = lax.broadcasted_iota(jnp.int32, (BLK, BLK), 0)
    col = lax.broadcasted_iota(jnp.int32, (BLK, BLK), 1)

    def listed(asks, key):
        found = jnp.where(cols[0, asks] == key, 1, 0)
        for n in range(1, 5):
            found = found + jnp.where(cols[n, asks] == key, 1, 0)
        return found

    def test(asks, key, same):
        return jnp.where((listed(asks, key) > 0) & same, 0.0, NEG)

    for i in range(2):
        at = slice(i * BLK, (i + 1) * BLK)
        own_keep = jnp.where(keep[pl.ds(blocks[3 + i], 1), :] == 1, 0.0, NEG)
        own_keep = jnp.broadcast_to(own_keep, (BLK, BLK)).T
        for e in range(8):
            same = owners[e] == owners[3 + i]
            line = jnp.where(keep[pl.ds(blocks[e], 1), :] == 1, 0.0, NEG)
            tile = jnp.broadcast_to(line + test(blocks[3 + i], blocks[e], same), (BLK, BLK))
            back = own_keep + test(blocks[e], blocks[3 + i], same)
            if e == 3 + i:
                tile = jnp.where(row == col, 0.0, tile)
                back = jnp.where(row == col, 0.0, back)
            bias[at, e * BLK : (e + 1) * BLK] = tile
            bias2[at, e * BLK : (e + 1) * BLK] = back
    for ref in (qh, kh, vh, dh):
        ref[...] = jnp.zeros_like(ref)
    mine = slice(3 * BLK, 5 * BLK)
    tok_t[...] = tw[mine, :].T
    cot_t[...] = ct[...].T
    for k in range(1, 4):
        for m in range(2):
            weights.far2(m, k)
    weights.finish()
    for copy in own_rows:
        copy.wait()

    dwin[3 * BLK : 5 * BLK, :] = dot(ct[...], wv[3].reshape(D, HH)).astype(BF16)

    def around(first, count):
        return dwin.at[pl.ds(first * BLK, count * BLK)]

    halo = [
        remote(around(4, 1), around(2, 1), sd.at[0], rd.at[0], up),
        remote(around(3, 1), around(5, 1), sd.at[1], rd.at[1], down),
        remote(around(3, 1), around(1, 1), sd.at[2], rd.at[2], up),
        remote(around(4, 1), around(6, 1), sd.at[3], rd.at[3], down),
    ]
    for copy in halo:
        copy.start()
    farther = [
        remote(around(2, 1), around(0, 1), sd.at[4], rd.at[4], up),
        remote(around(5, 1), around(7, 1), sd.at[5], rd.at[5], down),
    ]
    for copy in edges[2:]:
        copy.wait_recv()

    def project(step, carry):
        at = pl.ds(pl.multiple_of(step * OWN, OWN), OWN)
        rows_in = tw[at, :]
        for m, ref in ((1, kh), (2, vh)):
            full = dot(rows_in, wv[m].reshape(D, HH)).astype(BF16)
            for h in range(HEADS):
                ref[h, at, 0:HD] = full[:, h * HD : (h + 1) * HD]
        return carry

    def queries(first, count):
        at = slice(first * BLK, (first + count) * BLK)
        full = dot(tw[at, :], wv[0].reshape(D, HH)).astype(BF16)
        for h in range(HEADS):
            qh[h, at, 0:HD] = full[:, h * HD : (h + 1) * HD]

    lax.fori_loop(0, 4, project, 0)
    queries(3, 2)
    for h in range(HEADS):
        dh[h, 3 * BLK : 5 * BLK, 0:HD] = dwin[3 * BLK : 5 * BLK, h * HD : (h + 1) * HD]
    halo[0].wait_recv()
    farther[0].start()
    halo[1].wait_recv()
    farther[1].start()

    lane = lax.broadcasted_iota(jnp.int32, (OWN, BLK), 1)
    stat[...] = jnp.zeros_like(stat)

    def ask_head(h, carry):
        k, v, d = kh[h], vh[h], dh[h, mine, :]
        s = dot_t(qh[h, mine, :], k) * SCALE2 + bias[...]
        top = jnp.max(s, axis=1, keepdims=True)
        e = jnp.exp2(s - top)
        norm = jnp.sum(e, axis=1, keepdims=True)
        p = e * (1.0 / norm)
        o = dot(p.astype(BF16), v).astype(BF16)
        oh[h] = o
        delta = jnp.sum(d.astype(F32) * o.astype(F32), axis=1, keepdims=True)
        ds = (p * (dot_t(d, v) - delta)).astype(BF16)
        gh[h] = (dot(ds, k) * SCALE).astype(BF16)
        lse = top + jnp.log2(norm)
        stat[...] = jnp.where(lane == h, lse, jnp.where(lane == h + HEADS, delta, stat[...]))
        return carry

    lax.fori_loop(0, HEADS, ask_head, 0)

    for i in range(2):
        sw[3 + i] = stat[i * BLK : (i + 1) * BLK, :].T[0 : 2 * HEADS, :]
    stats = [
        remote(sw.at[pl.ds(3, 2)], sw.at[pl.ds(1, 2)], st.at[0], rt.at[0], up),
        remote(sw.at[pl.ds(3, 2)], sw.at[pl.ds(5, 2)], st.at[1], rt.at[1], down),
        remote(sw.at[4], sw.at[0], st.at[2], rt.at[2], up2),
        remote(sw.at[3], sw.at[7], st.at[3], rt.at[3], down2),
    ]
    for copy in stats:
        copy.start()

    early = Wave(refs[0], sems[0], seq, x, y, core)
    late = Wave(refs[1], sems[1], seq, x, y, core)

    def partial(dst, lhs, rhs):
        def part(r, carry):
            at = pl.ds(pl.multiple_of(r * 352, 352), 352)
            full = dot(lhs[at, :], rhs[...])
            for k in range(4):
                dst[4 * r + k] = full[k * CHIP : (k + 1) * CHIP, :].astype(BF16)
            return carry

        lax.fori_loop(0, 4, part, 0)

    for h in range(HEADS):
        att[:, h * HD : (h + 1) * HD] = oh[h, :, 0:HD]
        dq[:, h * HD : (h + 1) * HD] = gh[h, :, 0:HD]
    partial(early.g.at[0], tok_t, dq)
    partial(early.g.at[1], cot_t, att)
    early.share()
    queries(0, 3)
    queries(5, 3)

    halo[2].wait_recv()
    halo[3].wait_recv()
    farther[0].wait_recv()
    farther[1].wait_recv()
    for h in range(HEADS):
        dh[h, 0 : 3 * BLK, 0:HD] = dwin[0 : 3 * BLK, h * HD : (h + 1) * HD]
        dh[h, 5 * BLK : 8 * BLK, 0:HD] = dwin[5 * BLK : 8 * BLK, h * HD : (h + 1) * HD]
    early.first(0)
    early.first(1)
    for copy in stats:
        copy.wait_recv()
    for i in range(8):
        rows[:, i * BLK : (i + 1) * BLK] = sw[i]

    def give_head(h, carry):
        q, d = qh[h], dh[h]
        lse = rows[pl.ds(h, 1), :]
        delta = rows[pl.ds(h + HEADS, 1), :]
        s = dot_t(kh[h, mine, :], q) * SCALE2 + bias2[...]
        p = jnp.exp2(s - lse)
        ds = (p * (dot_t(vh[h, mine, :], d) - delta)).astype(BF16)
        vg[h] = dot(p.astype(BF16), d).astype(BF16)
        kg[h] = (dot(ds, q) * SCALE).astype(BF16)
        return carry

    lax.fori_loop(0, 2, give_head, 0)
    early.first(2)
    early.first(3)
    early.middle(0)
    lax.fori_loop(2, 4, give_head, 0)
    early.middle(1)
    lax.fori_loop(4, 6, give_head, 0)
    early.middle(2)
    early.middle(3)
    lax.fori_loop(6, 8, give_head, 0)
    for h in range(HEADS):
        dk[:, h * HD : (h + 1) * HD] = kg[h, :, 0:HD]
        dv[:, h * HD : (h + 1) * HD] = vg[h, :, 0:HD]
    partial(late.g.at[0], tok_t, dk)
    partial(late.g.at[1], tok_t, dv)
    late.share()
    early.last(0)
    out[...] = dot_t(att[...], wv[3].reshape(D, HH)).astype(BF16)
    early.last(1)
    late.first(0)
    early.last(2)
    late.first(1)
    late.middle(0)
    early.last(3)
    late.first(2)
    late.middle(1)
    early.spread(total)
    late.first(3)
    late.middle(2)
    late.last(0)
    late.middle(3)
    late.last(1)
    early.finish()
    late.last(2)
    late.last(3)
    early.pass_on()
    late.spread(total)
    gin[...] = (
        dot_t(dq[...], wv[0].reshape(D, HH))
        + dot_t(dk[...], wv[1].reshape(D, HH))
        + dot_t(dv[...], wv[2].reshape(D, HH))
    ).astype(BF16)
    early.collect(gout, 0, 3)
    late.finish()
    late.pass_on()
    late.collect(gout, 1, 2)
    for copy in halo + farther + stats + edges + weights.sends + swaps:
        copy.wait_send()


def sublayer(wsh, tok, cot, cols, cuts, keep):
    dma = pltpu.SemaphoreType.DMA
    grid16 = (NX * NY, CHIP, HH)
    heads, heads_own = (HEADS, WINDOW, BLK), (HEADS, OWN, BLK)
    bf = lambda *shape: pltpu.VMEM(shape, BF16)
    scratch = [bf(4, *grid16), bf(WINDOW, D), bf(OWN, D)]
    scratch += [bf(*heads)] * 4 + [bf(*heads_own)] * 4
    scratch += [
        bf(WINDOW, HH),
        pltpu.VMEM((OWN, WINDOW), F32),
        pltpu.VMEM((OWN, WINDOW), F32),
        pltpu.VMEM((OWN, BLK), F32),
        pltpu.VMEM((8, 2 * HEADS, BLK), F32),
        pltpu.VMEM((2 * HEADS, WINDOW), F32),
        bf(D, OWN),
        bf(D, OWN),
    ]
    scratch += [bf(OWN, HH)] * 4 + [pltpu.VMEM((CHIP, HH), F32)]
    scratch += [bf(2, wsh.shape[1], HH), bf(2, CHIP, HH)]
    for wave in range(2):
        scratch += [
            bf(2, *grid16),
            bf(*grid16),
            bf(4, CHIP, HH),
            bf(4, 2, CHIP, HH),
            bf(3, CHIP, HH),
            bf(8, 24, 384),
            bf(7, 24, 384),
            bf(2, 8, 24, 384),
        ]
    scratch += [dma((4,))] + [dma((6,))] * 2 + [dma((4,))] * 2
    for wave in range(2):
        for count in (16, 16, 3, 7, 7, 8):
            scratch += [dma((count,))] * 2
    for count in (2, 6, 8, 32, 32):
        scratch += [dma((count,))] * 2
    return pl.pallas_call(
        sublayer_kernel,
        out_shape=(
            jax.ShapeDtypeStruct((OWN, D), BF16),
            jax.ShapeDtypeStruct((OWN, D), BF16),
            jax.ShapeDtypeStruct((4, CHIP, HH), F32),
        ),
        in_specs=[VMEM, HBM, HBM, SMEM, SMEM, VMEM],
        out_specs=(VMEM,) * 3,
        scratch_shapes=scratch,
        compiler_params=pltpu.CompilerParams(
            collective_id=1, has_side_effects=True, vmem_limit_bytes=62 << 20
        ),
        name="sublayer",
    )(wsh, tok, cot, cols, cuts, keep)


def body(tokens, weights, cotangent, col_list, cut_lengths, keep_mask):
    core = lax.axis_index("dp") % 2
    shard = weights.shape[0]
    result, grad_in, summed = sublayer(
        jnp.transpose(weights, (1, 0, 2)),
        tokens[0],
        cotangent[0],
        col_list[0].T,
        cut_lengths[0],
        keep_mask[0].reshape(NBLK, BLK),
    )
    mine = lax.dynamic_slice(summed, (0, shard * core, 0), (4, shard, HH))
    return (result[None], grad_in[None], jnp.transpose(mine, (1, 0, 2)))


def solution(mesh):
    placed = (
        P("dp", "seq", None),
        P("dp", None, None),
        P("dp", "seq", None),
        P("dp", None, None),
        P("dp", None),
        P("dp", None),
    )
    return jax.shard_map(
        body,
        mesh=mesh,
        in_specs=placed,
        out_specs=(P("dp", "seq", None), P("dp", "seq", None), P("dp", None, None)),
        check_vma=False,
    )
```

```python
import math

import jax
import jax.numpy as jnp
from jax import lax
from jax.experimental import pallas as pl
from jax.experimental.pallas import tpu as pltpu
from jax.sharding import PartitionSpec as P

HD = 88
HEADS = 8
HH = 704
D = 1408
OWN = 256
WINDOW = 1024
BLK = 128
NBLK = 16
NX = 4
NY = 4
NZ = 8
CHIP = 88
CUT = 48
NEG = -1e30
MESH = pl.DeviceIdType.MESH
F32 = jnp.float32
BF16 = jnp.bfloat16
VMEM = pl.BlockSpec(memory_space=pltpu.VMEM)
HBM = pl.BlockSpec(memory_space=pltpu.HBM)
SMEM = pl.BlockSpec(memory_space=pltpu.SMEM)


def place():
    seq = lax.axis_index("seq")
    dp = lax.axis_index("dp")
    return seq, dp // (2 * NY), (dp // 2) % NY, dp % 2


def device(seq, x, y, core):
    return (seq, (x * NY + y) * 2 + core)


def greet(others):
    barrier = pltpu.get_barrier_semaphore()
    for other in others:
        pl.semaphore_signal(barrier, inc=1, device_id=other, device_id_type=MESH)
    pl.semaphore_wait(barrier, len(others))


def neighbours(seq, x, y, core):
    return [
        device(seq, x, y, 1 - core),
        device(seq, (x + 1) % NX, y, core),
        device(seq, (x + NX - 1) % NX, y, core),
        device(seq, x, (y + 1) % NY, core),
        device(seq, x, (y + NY - 1) % NY, core),
        device(seq, (x + 2) % NX, y, core),
        device(seq, x, (y + 2) % NY, core),
    ]


def remote(src, dst, send, recv, target):
    return pltpu.make_async_remote_copy(
        src_ref=src, dst_ref=dst, send_sem=send, recv_sem=recv, device_id=target, device_id_type=MESH
    )


NT = (((1,), (1,)), ((), ()))
SCALE = 1.0 / math.sqrt(HD)
SCALE2 = SCALE * math.log2(math.e)
ROWS = (0, 24, 48, 64)
COLS = (0, 320)
FAR_FIRST = (4, 3, 5, 2, 6, 1, 7)


def dot(lhs, rhs):
    return jnp.dot(lhs, rhs, preferred_element_type=F32)


def dot_t(lhs, rhs):
    return lax.dot_general(lhs, rhs, NT, preferred_element_type=F32)


class Gather:
    def __init__(self, wv, blk, sems, seq, x, y, core):
        self.wv, self.blk, self.sems = wv, blk, sems
        self.seq, self.core = seq, core
        self.a, self.b = (1 - core) * x + core * y, (1 - core) * y + core * x
        a, b = self.a, self.b
        self.order1 = (a, (a + 3) % 4, (a + 1) % 4, (a + 2) % 4)
        self.order2 = (b, (b + 3) % 4, (b + 1) % 4, (b + 2) % 4)
        self.other = device(seq, x, y, 1 - core)
        self.sends = []

    def rows(self, half, m, aa, bb, core, first=0, count=CHIP):
        p = (1 - core) * (aa * 4 + bb) + core * (bb * 4 + aa)
        return self.wv.at[2 * half + m, p, pl.ds(first, count)]

    def at(self, aa, bb):
        core = self.core
        return (self.seq, ((1 - core) * (aa * 4 + bb) + core * (bb * 4 + aa)) * 2 + core)

    def send(self, src, dst, kind, index, target):
        copy = remote(src, dst, self.sems[kind][0].at[index], self.sems[kind][1].at[index], target)
        copy.start()
        self.sends.append(copy)

    def arrived(self, dst, kind, index):
        remote(dst, dst, self.sems[kind][0].at[index], self.sems[kind][1].at[index], self.other).wait_recv()

    def mine(self, m, k, j, first=0, count=CHIP):
        return self.rows(self.core, m, self.order1[k], self.order2[j], self.core, first, count)

    def second(self, src, m, k):
        for i in range(2):
            self.send(src, self.mine(m, k, 0), "2", 16 * m + 4 * k + i, self.at(self.a, self.order2[2 - i]))

    def share(self, src, m, k, j):
        self.send(src, self.mine(m, k, j), "s", 16 * m + 4 * j + k, self.other)

    def start(self, m):
        src = self.blk.at[m]
        for i in range(2):
            self.send(src, self.mine(m, 0, 0), "1", 4 * m + i, self.at(self.order1[2 - i], self.b))
        self.second(src, m, 0)
        self.share(src, m, 0, 0)

    def near(self, m, i):
        block = self.mine(m, 1 + i, 0)
        self.arrived(block, "1", 4 * m + i)
        part = self.mine(m, 1 + i, 0, CUT * i, (CUT, CHIP - CUT)[i])
        self.send(part, part, "1", 4 * m + 2 + i, self.at(self.order1[2 - i], self.b))
        self.second(block, m, 1 + i)
        self.share(block, m, 1 + i, 0)

    def opposite(self, m):
        self.arrived(self.mine(m, 3, 0, 0, CUT), "1", 4 * m + 2)
        self.arrived(self.mine(m, 3, 0, CUT, CHIP - CUT), "1", 4 * m + 3)
        self.second(self.mine(m, 3, 0), m, 3)
        self.share(self.mine(m, 3, 0), m, 3, 0)

    def near2(self, m, k):
        for i in range(2):
            block = self.mine(m, k, 1 + i)
            self.arrived(block, "2", 16 * m + 4 * k + i)
            part = self.mine(m, k, 1 + i, CUT * i, (CUT, CHIP - CUT)[i])
            self.send(part, part, "2", 16 * m + 4 * k + 2 + i, self.at(self.a, self.order2[2 - i]))
            self.share(block, m, k, 1 + i)

    def far2(self, m, k):
        self.arrived(self.mine(m, k, 3, 0, CUT), "2", 16 * m + 4 * k + 2)
        self.arrived(self.mine(m, k, 3, CUT, CHIP - CUT), "2", 16 * m + 4 * k + 3)
        self.share(self.mine(m, k, 3), m, k, 3)

    def finish(self):
        core = self.core
        for m in range(2):
            for j in range(4):
                for k in range(4):
                    block = self.rows(1 - core, m, self.order2[k], self.order1[j], 1 - core)
                    self.arrived(block, "s", 16 * m + 4 * j + k)


class Wave:
    def __init__(self, refs, sems, seq, x, y, core):
        self.g, self.sib, self.p1, self.q1, self.q2, self.pieces, self.rz, self.zz = refs
        self.sems = sems
        self.seq, self.core = seq, core
        self.a, self.b = (1 - core) * x + core * y, (1 - core) * y + core * x
        a, b = self.a, self.b
        self.order1 = ((a + 2) % 4, (a + 1) % 4, (a + 3) % 4, a)
        self.order2 = ((b + 2) % 4, (b + 1) % 4, (b + 3) % 4, b)
        self.other = device(seq, x, y, 1 - core)
        self.peers = [device((seq + k) % NZ, x, y, core) for k in range(1, NZ)]
        self.sends = []

    def slot(self, aa, bb):
        return (1 - self.core) * (aa * 4 + bb) + self.core * (bb * 4 + aa)

    def at(self, aa, bb):
        return (self.seq, self.slot(aa, bb) * 2 + self.core)

    def send(self, src, dst, kind, index, target):
        copy = remote(src, dst, self.sems[kind][0].at[index], self.sems[kind][1].at[index], target)
        copy.start()
        self.sends.append(copy)

    def arrived(self, dst, kind, index):
        remote(dst, dst, self.sems[kind][0].at[index], self.sems[kind][1].at[index], self.other).wait_recv()

    def share(self):
        for j in range(4):
            for k in range(4):
                aa, bb = self.order2[k], self.order1[j]
                p = self.core * (aa * 4 + bb) + (1 - self.core) * (bb * 4 + aa)
                self.send(self.g.at[1 - self.core, p], self.sib.at[p], "s", 4 * j + k, self.other)

    def add(self, j, k):
        p = self.slot(self.order1[k], self.order2[j])
        self.arrived(self.sib.at[p], "s", 4 * j + k)
        self.g[self.core, p] = (self.g[self.core, p].astype(F32) + self.sib[p].astype(F32)).astype(BF16)

    def first(self, j):
        self.add(j, 0)
        far = self.g.at[self.core, self.slot(self.order1[0], self.order2[j])]
        for i, part in enumerate((pl.ds(0, CUT), pl.ds(CUT, CHIP - CUT))):
            self.send(far.at[part], self.p1.at[j, part], "1", 4 * j + i, self.at(self.order1[1 + i], self.b))
        for k in range(1, 4):
            self.add(j, k)

    def middle(self, j):
        for i, part in enumerate((pl.ds(0, CUT), pl.ds(CUT, CHIP - CUT))):
            near = self.g.at[self.core, self.slot(self.order1[1 + i], self.order2[j])]
            self.arrived(self.p1.at[j, part], "1", 4 * j + i)
            near[part] = (near[part].astype(F32) + self.p1[j, part].astype(F32)).astype(BF16)
            self.send(near, self.q1.at[j, i], "1", 4 * j + 2 + i, self.at(self.order1[1 + i], self.b))

    def last(self, j):
        own = self.g.at[self.core, self.slot(self.a, self.order2[j])]
        self.arrived(self.q1.at[j, 0], "1", 4 * j + 2)
        self.arrived(self.q1.at[j, 1], "1", 4 * j + 3)
        own[...] = (own[...].astype(F32) + self.q1[j, 0].astype(F32) + self.q1[j, 1].astype(F32)).astype(BF16)
        if j < 3:
            self.send(own, self.q2.at[j], "2", j, self.at(self.a, self.order2[j]))

    def spread(self, total):
        acc = self.g[self.core, self.slot(self.a, self.b)].astype(F32)
        for k in range(3):
            self.arrived(self.q2.at[k], "2", k)
            acc = acc + self.q2[k].astype(F32)
        total[...] = acc
        for piece in range(8):
            r0, c0 = ROWS[piece // 2], COLS[piece % 2]
            self.pieces[piece] = total[r0 : r0 + 24, c0 : c0 + 384].astype(BF16)
        for k in FAR_FIRST:
            target = (self.seq + k) % NZ
            self.send(self.pieces.at[target], self.rz.at[k - 1], "z", k - 1, self.peers[k - 1])

    def finish(self):
        acc = self.pieces[self.seq].astype(F32)
        for k in range(1, NZ):
            self.arrived(self.rz.at[k - 1], "z", k - 1)
            acc = acc + self.rz[k - 1].astype(F32)
        self.zz[self.core, self.seq] = acc.astype(BF16)
        mine = self.zz.at[self.core, self.seq]
        for k in FAR_FIRST:
            self.send(mine, mine, "g", k - 1, self.peers[k - 1])
        self.send(mine, mine, "w", 0, self.other)

    def pass_on(self):
        for k in FAR_FIRST[::-1]:
            piece = self.zz.at[self.core, (self.seq + NZ - k) % NZ]
            self.arrived(piece, "g", k - 1)
            self.send(piece, piece, "w", k, self.other)

    def collect(self, gout, first, second):
        for k in range(NZ):
            self.arrived(self.zz.at[1 - self.core, (self.seq + NZ - k) % NZ], "w", k)
        for m, index in enumerate((first, second)):
            for piece in range(8):
                r0, c0 = ROWS[piece // 2], COLS[piece % 2]
                gout[index, r0 : r0 + 24, c0 : c0 + 384] = self.zz[m, piece].astype(F32) * (1.0 / 32.0)
        for copy in self.sends:
            copy.wait_send()


def sublayer_kernel(
    wsh, tok, cot, cols, cuts, keep, out, gin, gout,
    wv, tw, ct, qh, kh, vh, dh, oh, gh, kg, vg, dwin, bias, bias2, stat, sw, rows, tok_t, cot_t, att, dq, dk, dv,
    total, sib, blk,
    *rest,
):
    refs = [rest[:8], rest[8:16]]
    ld, sd, rd, st, rt = rest[16:21]
    sems = []
    for wave in range(2):
        flat = rest[21 + 12 * wave : 33 + 12 * wave]
        sems.append({kind: (flat[2 * i], flat[2 * i + 1]) for i, kind in enumerate("s12zgw")})
    flat = rest[45:]
    gather_sems = {kind: (flat[2 * i], flat[2 * i + 1]) for i, kind in enumerate("xt12s")}
    seq, x, y, core = place()
    other = device(seq, x, y, 1 - core)
    up, down = device((seq + 1) % NZ, x, y, core), device((seq + NZ - 1) % NZ, x, y, core)
    up2, down2 = device((seq + 2) % NZ, x, y, core), device((seq + NZ - 2) % NZ, x, y, core)

    def halo_rows(first, count):
        return tw.at[pl.ds(first * BLK, count * BLK)]

    load_cot = pltpu.make_async_copy(cot, ct, ld.at[0])
    load_tok = pltpu.make_async_copy(tok, halo_rows(3, 2), ld.at[1])
    load_cot.start()
    load_tok.start()
    greet(neighbours(seq, x, y, core) + [device((seq + k) % NZ, x, y, core) for k in range(1, NZ)])

    swaps = []
    for m in range(2):
        xsend, xrecv = gather_sems["x"]
        swaps.append(remote(wsh.at[2 * (1 - core) + m], sib.at[m], xsend.at[m], xrecv.at[m], other))
        swaps[m].start()
    low, high = tok.at[pl.ds(0, BLK)], tok.at[pl.ds(BLK, BLK)]
    tsend, trecv = gather_sems["t"]
    edges = [
        remote(high, halo_rows(2, 1), tsend.at[0], trecv.at[0], up),
        remote(low, halo_rows(5, 1), tsend.at[1], trecv.at[1], down),
        remote(low, halo_rows(1, 1), tsend.at[2], trecv.at[2], up),
        remote(high, halo_rows(6, 1), tsend.at[3], trecv.at[3], down),
    ]
    for copy in edges:
        copy.start()
    edges += [
        remote(halo_rows(2, 1), halo_rows(0, 1), tsend.at[4], trecv.at[4], up),
        remote(halo_rows(5, 1), halo_rows(7, 1), tsend.at[5], trecv.at[5], down),
    ]
    weights = Gather(wv, blk, gather_sems, seq, x, y, core)
    own_rows = []
    for m in range(2):
        swaps[m].wait_recv()
        ours = wsh[2 * core + m]
        theirs = sib[m]
        shard = ours.shape[0]
        blk[m, 0:shard, :] = jnp.where(core == 0, ours, theirs)
        blk[m, shard:CHIP, :] = jnp.where(core == 0, theirs, ours)
        own_rows.append(pltpu.make_async_copy(blk.at[m], weights.mine(m, 0, 0), ld.at[2 + m]))
        own_rows[m].start()
        weights.start(m)

    for m in range(2):
        weights.near(m, 0)
        weights.near(m, 1)
        weights.near2(m, 0)
    for m in range(2):
        weights.opposite(m)
    weights.near2(0, 1)
    weights.near2(1, 1)
    weights.far2(0, 0)
    weights.near2(0, 2)
    weights.far2(1, 0)
    weights.near2(1, 2)
    edges[0].wait_recv()
    edges[4].start()
    edges[1].wait_recv()
    edges[5].start()
    weights.near2(0, 3)
    weights.near2(1, 3)
    load_cot.wait()
    load_tok.wait()
    blocks = [(2 * seq + NBLK - 3 + i) % NBLK for i in range(8)]
    ends = []
    for c in range(5):
        ends.append(cuts[c] if c == 0 else ends[-1] + cuts[c])

    def owner(index):
        return sum([jnp.where(end <= index, 1, 0) for end in ends])

    owners = [owner(e) for e in blocks]
    row = lax.broadcasted_iota(jnp.int32, (BLK, BLK), 0)
    col = lax.broadcasted_iota(jnp.int32, (BLK, BLK), 1)

    def listed(asks, key):
        found = jnp.where(cols[0, asks] == key, 1, 0)
        for n in range(1, 5):
            found = found + jnp.where(cols[n, asks] == key, 1, 0)
        return found

    def test(asks, key, same):
        return jnp.where((listed(asks, key) > 0) & same, 0.0, NEG)

    for i in range(2):
        at = slice(i * BLK, (i + 1) * BLK)
        own_keep = jnp.where(keep[pl.ds(blocks[3 + i], 1), :] == 1, 0.0, NEG)
        own_keep = jnp.broadcast_to(own_keep, (BLK, BLK)).T
        for e in range(8):
            same = owners[e] == owners[3 + i]
            line = jnp.where(keep[pl.ds(blocks[e], 1), :] == 1, 0.0, NEG)
            tile = jnp.broadcast_to(line + test(blocks[3 + i], blocks[e], same), (BLK, BLK))
            back = own_keep + test(blocks[e], blocks[3 + i], same)
            if e == 3 + i:
                tile = jnp.where(row == col, 0.0, tile)
                back = jnp.where(row == col, 0.0, back)
            bias[at, e * BLK : (e + 1) * BLK] = tile
            bias2[at, e * BLK : (e + 1) * BLK] = back
    for ref in (qh, kh, vh, dh):
        ref[...] = jnp.zeros_like(ref)
    mine = slice(3 * BLK, 5 * BLK)
    tok_t[...] = tw[mine, :].T
    cot_t[...] = ct[...].T
    for k in range(1, 4):
        for m in range(2):
            weights.far2(m, k)
    weights.finish()
    for copy in own_rows:
        copy.wait()

    dwin[3 * BLK : 5 * BLK, :] = dot(ct[...], wv[3].reshape(D, HH)).astype(BF16)

    def around(first, count):
        return dwin.at[pl.ds(first * BLK, count * BLK)]

    halo = [
        remote(around(4, 1), around(2, 1), sd.at[0], rd.at[0], up),
        remote(around(3, 1), around(5, 1), sd.at[1], rd.at[1], down),
        remote(around(3, 1), around(1, 1), sd.at[2], rd.at[2], up),
        remote(around(4, 1), around(6, 1), sd.at[3], rd.at[3], down),
    ]
    for copy in halo:
        copy.start()
    farther = [
        remote(around(2, 1), around(0, 1), sd.at[4], rd.at[4], up),
        remote(around(5, 1), around(7, 1), sd.at[5], rd.at[5], down),
    ]
    for copy in edges[2:]:
        copy.wait_recv()

    def project(step, carry):
        at = pl.ds(pl.multiple_of(step * OWN, OWN), OWN)
        rows_in = tw[at, :]
        for m, ref in ((1, kh), (2, vh)):
            full = dot(rows_in, wv[m].reshape(D, HH)).astype(BF16)
            for h in range(HEADS):
                ref[h, at, 0:HD] = full[:, h * HD : (h + 1) * HD]
        return carry

    def queries(first, count):
        at = slice(first * BLK, (first + count) * BLK)
        full = dot(tw[at, :], wv[0].reshape(D, HH)).astype(BF16)
        for h in range(HEADS):
            qh[h, at, 0:HD] = full[:, h * HD : (h + 1) * HD]

    lax.fori_loop(0, 4, project, 0)
    queries(3, 2)
    for h in range(HEADS):
        dh[h, 3 * BLK : 5 * BLK, 0:HD] = dwin[3 * BLK : 5 * BLK, h * HD : (h + 1) * HD]
    halo[0].wait_recv()
    farther[0].start()
    halo[1].wait_recv()
    farther[1].start()

    lane = lax.broadcasted_iota(jnp.int32, (OWN, BLK), 1)
    stat[...] = jnp.zeros_like(stat)

    def ask_head(h, carry):
        k, v, d = kh[h], vh[h], dh[h, mine, :]
        s = dot_t(qh[h, mine, :], k) * SCALE2 + bias[...]
        top = jnp.max(s, axis=1, keepdims=True)
        e = jnp.exp2(s - top)
        norm = jnp.sum(e, axis=1, keepdims=True)
        p = e * (1.0 / norm)
        o = dot(p.astype(BF16), v).astype(BF16)
        oh[h] = o
        delta = jnp.sum(d.astype(F32) * o.astype(F32), axis=1, keepdims=True)
        ds = (p * (dot_t(d, v) - delta)).astype(BF16)
        gh[h] = (dot(ds, k) * SCALE).astype(BF16)
        lse = top + jnp.log2(norm)
        stat[...] = jnp.where(lane == h, lse, jnp.where(lane == h + HEADS, delta, stat[...]))
        return carry

    lax.fori_loop(0, HEADS, ask_head, 0)

    for i in range(2):
        sw[3 + i] = stat[i * BLK : (i + 1) * BLK, :].T[0 : 2 * HEADS, :]
    stats = [
        remote(sw.at[pl.ds(3, 2)], sw.at[pl.ds(1, 2)], st.at[0], rt.at[0], up),
        remote(sw.at[pl.ds(3, 2)], sw.at[pl.ds(5, 2)], st.at[1], rt.at[1], down),
        remote(sw.at[4], sw.at[0], st.at[2], rt.at[2], up2),
        remote(sw.at[3], sw.at[7], st.at[3], rt.at[3], down2),
    ]
    for copy in stats:
        copy.start()

    early = Wave(refs[0], sems[0], seq, x, y, core)
    late = Wave(refs[1], sems[1], seq, x, y, core)

    def partial(dst, lhs, rhs):
        def part(r, carry):
            at = pl.ds(pl.multiple_of(r * 352, 352), 352)
            full = dot(lhs[at, :], rhs[...])
            for k in range(4):
                dst[4 * r + k] = full[k * CHIP : (k + 1) * CHIP, :].astype(BF16)
            return carry

        lax.fori_loop(0, 4, part, 0)

    for h in range(HEADS):
        att[:, h * HD : (h + 1) * HD] = oh[h, :, 0:HD]
        dq[:, h * HD : (h + 1) * HD] = gh[h, :, 0:HD]
    partial(early.g.at[0], tok_t, dq)
    partial(early.g.at[1], cot_t, att)
    early.share()
    queries(0, 3)
    queries(5, 3)

    halo[2].wait_recv()
    halo[3].wait_recv()
    farther[0].wait_recv()
    farther[1].wait_recv()
    for h in range(HEADS):
        dh[h, 0 : 3 * BLK, 0:HD] = dwin[0 : 3 * BLK, h * HD : (h + 1) * HD]
        dh[h, 5 * BLK : 8 * BLK, 0:HD] = dwin[5 * BLK : 8 * BLK, h * HD : (h + 1) * HD]
    early.first(0)
    early.first(1)
    for copy in stats:
        copy.wait_recv()
    for i in range(8):
        rows[:, i * BLK : (i + 1) * BLK] = sw[i]

    def give_head(h, carry):
        q, d = qh[h], dh[h]
        lse = rows[pl.ds(h, 1), :]
        delta = rows[pl.ds(h + HEADS, 1), :]
        s = dot_t(kh[h, mine, :], q) * SCALE2 + bias2[...]
        p = jnp.exp2(s - lse)
        ds = (p * (dot_t(vh[h, mine, :], d) - delta)).astype(BF16)
        vg[h] = dot(p.astype(BF16), d).astype(BF16)
        kg[h] = (dot(ds, q) * SCALE).astype(BF16)
        return carry

    lax.fori_loop(0, 2, give_head, 0)
    early.first(2)
    early.first(3)
    early.middle(0)
    lax.fori_loop(2, 4, give_head, 0)
    early.middle(1)
    lax.fori_loop(4, 6, give_head, 0)
    early.middle(2)
    early.middle(3)
    lax.fori_loop(6, 8, give_head, 0)
    for h in range(HEADS):
        dk[:, h * HD : (h + 1) * HD] = kg[h, :, 0:HD]
        dv[:, h * HD : (h + 1) * HD] = vg[h, :, 0:HD]
    partial(late.g.at[0], tok_t, dk)
    partial(late.g.at[1], tok_t, dv)
    late.share()
    early.last(0)
    out[...] = dot_t(att[...], wv[3].reshape(D, HH)).astype(BF16)
    early.last(1)
    late.first(0)
    early.last(2)
    late.first(1)
    late.middle(0)
    early.last(3)
    late.first(2)
    late.middle(1)
    early.spread(total)
    late.first(3)
    late.middle(2)
    late.last(0)
    late.middle(3)
    late.last(1)
    early.finish()
    late.last(2)
    late.last(3)
    early.pass_on()
    late.spread(total)
    gin[...] = (
        dot_t(dq[...], wv[0].reshape(D, HH))
        + dot_t(dk[...], wv[1].reshape(D, HH))
        + dot_t(dv[...], wv[2].reshape(D, HH))
    ).astype(BF16)
    late.finish()
    early.collect(gout, 0, 3)
    late.pass_on()
    late.collect(gout, 1, 2)
    for copy in halo + farther + stats + edges + weights.sends + swaps:
        copy.wait_send()


def sublayer(wsh, tok, cot, cols, cuts, keep):
    dma = pltpu.SemaphoreType.DMA
    grid16 = (NX * NY, CHIP, HH)
    heads, heads_own = (HEADS, WINDOW, BLK), (HEADS, OWN, BLK)
    bf = lambda *shape: pltpu.VMEM(shape, BF16)
    scratch = [bf(4, *grid16), bf(WINDOW, D), bf(OWN, D)]
    scratch += [bf(*heads)] * 4 + [bf(*heads_own)] * 4
    scratch += [
        bf(WINDOW, HH),
        pltpu.VMEM((OWN, WINDOW), F32),
        pltpu.VMEM((OWN, WINDOW), F32),
        pltpu.VMEM((OWN, BLK), F32),
        pltpu.VMEM((8, 2 * HEADS, BLK), F32),
        pltpu.VMEM((2 * HEADS, WINDOW), F32),
        bf(D, OWN),
        bf(D, OWN),
    ]
    scratch += [bf(OWN, HH)] * 4 + [pltpu.VMEM((CHIP, HH), F32)]
    scratch += [bf(2, wsh.shape[1], HH), bf(2, CHIP, HH)]
    for wave in range(2):
        scratch += [
            bf(2, *grid16),
            bf(*grid16),
            bf(4, CHIP, HH),
            bf(4, 2, CHIP, HH),
            bf(3, CHIP, HH),
            bf(8, 24, 384),
            bf(7, 24, 384),
            bf(2, 8, 24, 384),
        ]
    scratch += [dma((4,))] + [dma((6,))] * 2 + [dma((4,))] * 2
    for wave in range(2):
        for count in (16, 16, 3, 7, 7, 8):
            scratch += [dma((count,))] * 2
    for count in (2, 6, 8, 32, 32):
        scratch += [dma((count,))] * 2
    return pl.pallas_call(
        sublayer_kernel,
        out_shape=(
            jax.ShapeDtypeStruct((OWN, D), BF16),
            jax.ShapeDtypeStruct((OWN, D), BF16),
            jax.ShapeDtypeStruct((4, CHIP, HH), F32),
        ),
        in_specs=[VMEM, HBM, HBM, SMEM, SMEM, VMEM],
        out_specs=(VMEM,) * 3,
        scratch_shapes=scratch,
        compiler_params=pltpu.CompilerParams(
            collective_id=1, has_side_effects=True, vmem_limit_bytes=62 << 20
        ),
        name="sublayer",
    )(wsh, tok, cot, cols, cuts, keep)


def body(tokens, weights, cotangent, col_list, cut_lengths, keep_mask):
    core = lax.axis_index("dp") % 2
    shard = weights.shape[0]
    result, grad_in, summed = sublayer(
        jnp.transpose(weights, (1, 0, 2)),
        tokens[0],
        cotangent[0],
        col_list[0].T,
        cut_lengths[0],
        keep_mask[0].reshape(NBLK, BLK),
    )
    mine = lax.dynamic_slice(summed, (0, shard * core, 0), (4, shard, HH))
    return (result[None], grad_in[None], jnp.transpose(mine, (1, 0, 2)))


def solution(mesh):
    placed = (
        P("dp", "seq", None),
        P("dp", None, None),
        P("dp", "seq", None),
        P("dp", None, None),
        P("dp", None),
        P("dp", None),
    )
    return jax.shard_map(
        body,
        mesh=mesh,
        in_specs=placed,
        out_specs=(P("dp", "seq", None), P("dp", "seq", None), P("dp", None, None)),
        check_vma=False,
    )
```

```python
import math

import jax
import jax.numpy as jnp
from jax import lax
from jax.experimental import pallas as pl
from jax.experimental.pallas import tpu as pltpu
from jax.sharding import PartitionSpec as P

HD = 88
HEADS = 8
HH = 704
D = 1408
OWN = 256
WINDOW = 1024
BLK = 128
NBLK = 16
NX = 4
NY = 4
NZ = 8
CHIP = 88
CUT = 48
NEG = -1e30
MESH = pl.DeviceIdType.MESH
F32 = jnp.float32
BF16 = jnp.bfloat16
VMEM = pl.BlockSpec(memory_space=pltpu.VMEM)
HBM = pl.BlockSpec(memory_space=pltpu.HBM)
SMEM = pl.BlockSpec(memory_space=pltpu.SMEM)


def place():
    seq = lax.axis_index("seq")
    dp = lax.axis_index("dp")
    return seq, dp // (2 * NY), (dp // 2) % NY, dp % 2


def device(seq, x, y, core):
    return (seq, (x * NY + y) * 2 + core)


def greet(others):
    barrier = pltpu.get_barrier_semaphore()
    for other in others:
        pl.semaphore_signal(barrier, inc=1, device_id=other, device_id_type=MESH)
    pl.semaphore_wait(barrier, len(others))


def neighbours(seq, x, y, core):
    return [
        device(seq, x, y, 1 - core),
        device(seq, (x + 1) % NX, y, core),
        device(seq, (x + NX - 1) % NX, y, core),
        device(seq, x, (y + 1) % NY, core),
        device(seq, x, (y + NY - 1) % NY, core),
        device(seq, (x + 2) % NX, y, core),
        device(seq, x, (y + 2) % NY, core),
    ]


def remote(src, dst, send, recv, target):
    return pltpu.make_async_remote_copy(
        src_ref=src, dst_ref=dst, send_sem=send, recv_sem=recv, device_id=target, device_id_type=MESH
    )


NT = (((1,), (1,)), ((), ()))
SCALE = 1.0 / math.sqrt(HD)
SCALE2 = SCALE * math.log2(math.e)
ROWS = (0, 24, 48, 64)
COLS = (0, 320)
FAR_FIRST = (4, 3, 5, 2, 6, 1, 7)


def dot(lhs, rhs):
    return jnp.dot(lhs, rhs, preferred_element_type=F32)


def dot_t(lhs, rhs):
    return lax.dot_general(lhs, rhs, NT, preferred_element_type=F32)


class Gather:
    def __init__(self, wv, blk, sems, seq, x, y, core):
        self.wv, self.blk, self.sems = wv, blk, sems
        self.seq, self.core = seq, core
        self.a, self.b = (1 - core) * x + core * y, (1 - core) * y + core * x
        a, b = self.a, self.b
        self.order1 = (a, (a + 3) % 4, (a + 1) % 4, (a + 2) % 4)
        self.order2 = (b, (b + 3) % 4, (b + 1) % 4, (b + 2) % 4)
        self.other = device(seq, x, y, 1 - core)
        self.sends = []

    def rows(self, half, m, aa, bb, core, first=0, count=CHIP):
        p = (1 - core) * (aa * 4 + bb) + core * (bb * 4 + aa)
        return self.wv.at[2 * half + m, p, pl.ds(first, count)]

    def at(self, aa, bb):
        core = self.core
        return (self.seq, ((1 - core) * (aa * 4 + bb) + core * (bb * 4 + aa)) * 2 + core)

    def send(self, src, dst, kind, index, target):
        copy = remote(src, dst, self.sems[kind][0].at[index], self.sems[kind][1].at[index], target)
        copy.start()
        self.sends.append(copy)

    def arrived(self, dst, kind, index):
        remote(dst, dst, self.sems[kind][0].at[index], self.sems[kind][1].at[index], self.other).wait_recv()

    def mine(self, m, k, j, first=0, count=CHIP):
        return self.rows(self.core, m, self.order1[k], self.order2[j], self.core, first, count)

    def second(self, src, m, k):
        for i in range(2):
            self.send(src, self.mine(m, k, 0), "2", 16 * m + 4 * k + i, self.at(self.a, self.order2[2 - i]))

    def share(self, src, m, k, j):
        self.send(src, self.mine(m, k, j), "s", 16 * m + 4 * j + k, self.other)

    def start(self, m):
        src = self.blk.at[m]
        for i in range(2):
            self.send(src, self.mine(m, 0, 0), "1", 4 * m + i, self.at(self.order1[2 - i], self.b))
        self.second(src, m, 0)
        self.share(src, m, 0, 0)

    def near(self, m, i):
        block = self.mine(m, 1 + i, 0)
        self.arrived(block, "1", 4 * m + i)
        part = self.mine(m, 1 + i, 0, CUT * i, (CUT, CHIP - CUT)[i])
        self.send(part, part, "1", 4 * m + 2 + i, self.at(self.order1[2 - i], self.b))
        self.second(block, m, 1 + i)
        self.share(block, m, 1 + i, 0)

    def opposite(self, m):
        self.arrived(self.mine(m, 3, 0, 0, CUT), "1", 4 * m + 2)
        self.arrived(self.mine(m, 3, 0, CUT, CHIP - CUT), "1", 4 * m + 3)
        self.second(self.mine(m, 3, 0), m, 3)
        self.share(self.mine(m, 3, 0), m, 3, 0)

    def near2(self, m, k):
        for i in range(2):
            block = self.mine(m, k, 1 + i)
            self.arrived(block, "2", 16 * m + 4 * k + i)
            part = self.mine(m, k, 1 + i, CUT * i, (CUT, CHIP - CUT)[i])
            self.send(part, part, "2", 16 * m + 4 * k + 2 + i, self.at(self.a, self.order2[2 - i]))
            self.share(block, m, k, 1 + i)

    def far2(self, m, k):
        self.arrived(self.mine(m, k, 3, 0, CUT), "2", 16 * m + 4 * k + 2)
        self.arrived(self.mine(m, k, 3, CUT, CHIP - CUT), "2", 16 * m + 4 * k + 3)
        self.share(self.mine(m, k, 3), m, k, 3)

    def finish(self):
        core = self.core
        for m in range(2):
            for j in range(4):
                for k in range(4):
                    block = self.rows(1 - core, m, self.order2[k], self.order1[j], 1 - core)
                    self.arrived(block, "s", 16 * m + 4 * j + k)


class Wave:
    def __init__(self, refs, sems, seq, x, y, core):
        self.g, self.sib, self.p1, self.q1, self.q2, self.pieces, self.rz, self.zz = refs
        self.sems = sems
        self.seq, self.core = seq, core
        self.a, self.b = (1 - core) * x + core * y, (1 - core) * y + core * x
        a, b = self.a, self.b
        self.order1 = ((a + 2) % 4, (a + 1) % 4, (a + 3) % 4, a)
        self.order2 = ((b + 2) % 4, (b + 1) % 4, (b + 3) % 4, b)
        self.other = device(seq, x, y, 1 - core)
        self.peers = [device((seq + k) % NZ, x, y, core) for k in range(1, NZ)]
        self.sends = []

    def slot(self, aa, bb):
        return (1 - self.core) * (aa * 4 + bb) + self.core * (bb * 4 + aa)

    def at(self, aa, bb):
        return (self.seq, self.slot(aa, bb) * 2 + self.core)

    def send(self, src, dst, kind, index, target):
        copy = remote(src, dst, self.sems[kind][0].at[index], self.sems[kind][1].at[index], target)
        copy.start()
        self.sends.append(copy)

    def arrived(self, dst, kind, index):
        remote(dst, dst, self.sems[kind][0].at[index], self.sems[kind][1].at[index], self.other).wait_recv()

    def share(self):
        for j in range(4):
            for k in range(4):
                aa, bb = self.order2[k], self.order1[j]
                p = self.core * (aa * 4 + bb) + (1 - self.core) * (bb * 4 + aa)
                self.send(self.g.at[1 - self.core, p], self.sib.at[p], "s", 4 * j + k, self.other)

    def add(self, j, k):
        p = self.slot(self.order1[k], self.order2[j])
        self.arrived(self.sib.at[p], "s", 4 * j + k)
        self.g[self.core, p] = (self.g[self.core, p].astype(F32) + self.sib[p].astype(F32)).astype(BF16)

    def first(self, j):
        self.add(j, 0)
        far = self.g.at[self.core, self.slot(self.order1[0], self.order2[j])]
        for i, part in enumerate((pl.ds(0, CUT), pl.ds(CUT, CHIP - CUT))):
            self.send(far.at[part], self.p1.at[j, part], "1", 4 * j + i, self.at(self.order1[1 + i], self.b))
        for k in range(1, 4):
            self.add(j, k)

    def middle(self, j):
        for i, part in enumerate((pl.ds(0, CUT), pl.ds(CUT, CHIP - CUT))):
            near = self.g.at[self.core, self.slot(self.order1[1 + i], self.order2[j])]
            self.arrived(self.p1.at[j, part], "1", 4 * j + i)
            near[part] = (near[part].astype(F32) + self.p1[j, part].astype(F32)).astype(BF16)
            self.send(near, self.q1.at[j, i], "1", 4 * j + 2 + i, self.at(self.order1[1 + i], self.b))

    def last(self, j):
        own = self.g.at[self.core, self.slot(self.a, self.order2[j])]
        self.arrived(self.q1.at[j, 0], "1", 4 * j + 2)
        self.arrived(self.q1.at[j, 1], "1", 4 * j + 3)
        own[...] = (own[...].astype(F32) + self.q1[j, 0].astype(F32) + self.q1[j, 1].astype(F32)).astype(BF16)
        if j < 3:
            self.send(own, self.q2.at[j], "2", j, self.at(self.a, self.order2[j]))

    def spread(self, total):
        acc = self.g[self.core, self.slot(self.a, self.b)].astype(F32)
        for k in range(3):
            self.arrived(self.q2.at[k], "2", k)
            acc = acc + self.q2[k].astype(F32)
        total[...] = acc
        for piece in range(8):
            r0, c0 = ROWS[piece // 2], COLS[piece % 2]
            self.pieces[piece] = total[r0 : r0 + 24, c0 : c0 + 384].astype(BF16)
        for k in FAR_FIRST:
            target = (self.seq + k) % NZ
            self.send(self.pieces.at[target], self.rz.at[k - 1], "z", k - 1, self.peers[k - 1])

    def finish(self):
        acc = self.pieces[self.seq].astype(F32)
        for k in range(1, NZ):
            self.arrived(self.rz.at[k - 1], "z", k - 1)
            acc = acc + self.rz[k - 1].astype(F32)
        self.zz[self.core, self.seq] = acc.astype(BF16)
        mine = self.zz.at[self.core, self.seq]
        for k in FAR_FIRST:
            self.send(mine, mine, "g", k - 1, self.peers[k - 1])
        self.send(mine, mine, "w", 0, self.other)

    def pass_on(self):
        for k in FAR_FIRST[::-1]:
            piece = self.zz.at[self.core, (self.seq + NZ - k) % NZ]
            self.arrived(piece, "g", k - 1)
            self.send(piece, piece, "w", k, self.other)

    def collect(self, gout, first, second):
        for k in range(NZ):
            self.arrived(self.zz.at[1 - self.core, (self.seq + NZ - k) % NZ], "w", k)
        for m, index in enumerate((first, second)):
            for piece in range(8):
                r0, c0 = ROWS[piece // 2], COLS[piece % 2]
                gout[index, r0 : r0 + 24, c0 : c0 + 384] = self.zz[m, piece].astype(F32) * (1.0 / 32.0)
        for copy in self.sends:
            copy.wait_send()


def sublayer_kernel(
    wsh, tok, cot, cols, cuts, keep, out, gin, gout,
    wv, tw, ct, qh, kh, vh, dh, oh, gh, kg, vg, dwin, bias, bias2, stat, sw, rows, tok_t, cot_t, att, dq, dk, dv,
    total, sib, blk,
    *rest,
):
    refs = [rest[:8], rest[8:16]]
    ld, sd, rd, st, rt = rest[16:21]
    sems = []
    for wave in range(2):
        flat = rest[21 + 12 * wave : 33 + 12 * wave]
        sems.append({kind: (flat[2 * i], flat[2 * i + 1]) for i, kind in enumerate("s12zgw")})
    flat = rest[45:]
    gather_sems = {kind: (flat[2 * i], flat[2 * i + 1]) for i, kind in enumerate("xt12s")}
    seq, x, y, core = place()
    other = device(seq, x, y, 1 - core)
    up, down = device((seq + 1) % NZ, x, y, core), device((seq + NZ - 1) % NZ, x, y, core)
    up2, down2 = device((seq + 2) % NZ, x, y, core), device((seq + NZ - 2) % NZ, x, y, core)

    def halo_rows(first, count):
        return tw.at[pl.ds(first * BLK, count * BLK)]

    load_cot = pltpu.make_async_copy(cot, ct, ld.at[0])
    load_tok = pltpu.make_async_copy(tok, halo_rows(3, 2), ld.at[1])
    load_cot.start()
    load_tok.start()
    greet(neighbours(seq, x, y, core) + [device((seq + k) % NZ, x, y, core) for k in range(1, NZ)])

    swaps = []
    for m in range(2):
        xsend, xrecv = gather_sems["x"]
        swaps.append(remote(wsh.at[2 * (1 - core) + m], sib.at[m], xsend.at[m], xrecv.at[m], other))
        swaps[m].start()
    low, high = tok.at[pl.ds(0, BLK)], tok.at[pl.ds(BLK, BLK)]
    tsend, trecv = gather_sems["t"]
    edges = [
        remote(high, halo_rows(2, 1), tsend.at[0], trecv.at[0], up),
        remote(low, halo_rows(5, 1), tsend.at[1], trecv.at[1], down),
        remote(low, halo_rows(1, 1), tsend.at[2], trecv.at[2], up),
        remote(high, halo_rows(6, 1), tsend.at[3], trecv.at[3], down),
    ]
    for copy in edges:
        copy.start()
    edges += [
        remote(halo_rows(2, 1), halo_rows(0, 1), tsend.at[4], trecv.at[4], up),
        remote(halo_rows(5, 1), halo_rows(7, 1), tsend.at[5], trecv.at[5], down),
    ]
    weights = Gather(wv, blk, gather_sems, seq, x, y, core)
    own_rows = []
    for m in range(2):
        swaps[m].wait_recv()
        ours = wsh[2 * core + m]
        theirs = sib[m]
        shard = ours.shape[0]
        blk[m, 0:shard, :] = jnp.where(core == 0, ours, theirs)
        blk[m, shard:CHIP, :] = jnp.where(core == 0, theirs, ours)
        own_rows.append(pltpu.make_async_copy(blk.at[m], weights.mine(m, 0, 0), ld.at[2 + m]))
        own_rows[m].start()
        weights.start(m)

    for m in range(2):
        weights.near(m, 0)
        weights.near(m, 1)
        weights.near2(m, 0)
    for m in range(2):
        weights.opposite(m)
    weights.near2(0, 1)
    weights.near2(1, 1)
    weights.far2(0, 0)
    weights.near2(0, 2)
    weights.far2(1, 0)
    weights.near2(1, 2)
    edges[0].wait_recv()
    edges[4].start()
    edges[1].wait_recv()
    edges[5].start()
    weights.near2(0, 3)
    weights.near2(1, 3)
    load_cot.wait()
    load_tok.wait()
    blocks = [(2 * seq + NBLK - 3 + i) % NBLK for i in range(8)]
    ends = []
    for c in range(5):
        ends.append(cuts[c] if c == 0 else ends[-1] + cuts[c])

    def owner(index):
        return sum([jnp.where(end <= index, 1, 0) for end in ends])

    owners = [owner(e) for e in blocks]
    row = lax.broadcasted_iota(jnp.int32, (BLK, BLK), 0)
    col = lax.broadcasted_iota(jnp.int32, (BLK, BLK), 1)

    def listed(asks, key):
        found = jnp.where(cols[0, asks] == key, 1, 0)
        for n in range(1, 5):
            found = found + jnp.where(cols[n, asks] == key, 1, 0)
        return found

    def test(asks, key, same):
        return jnp.where((listed(asks, key) > 0) & same, 0.0, NEG)

    for i in range(2):
        at = slice(i * BLK, (i + 1) * BLK)
        own_keep = jnp.where(keep[pl.ds(blocks[3 + i], 1), :] == 1, 0.0, NEG)
        own_keep = jnp.broadcast_to(own_keep, (BLK, BLK)).T
        for e in range(8):
            same = owners[e] == owners[3 + i]
            line = jnp.where(keep[pl.ds(blocks[e], 1), :] == 1, 0.0, NEG)
            tile = jnp.broadcast_to(line + test(blocks[3 + i], blocks[e], same), (BLK, BLK))
            back = own_keep + test(blocks[e], blocks[3 + i], same)
            if e == 3 + i:
                tile = jnp.where(row == col, 0.0, tile)
                back = jnp.where(row == col, 0.0, back)
            bias[at, e * BLK : (e + 1) * BLK] = tile
            bias2[at, e * BLK : (e + 1) * BLK] = back
    for ref in (qh, kh, vh, dh):
        ref[...] = jnp.zeros_like(ref)
    mine = slice(3 * BLK, 5 * BLK)
    tok_t[...] = tw[mine, :].T
    cot_t[...] = ct[...].T
    for k in range(1, 4):
        for m in range(2):
            weights.far2(m, k)
    weights.finish()
    for copy in own_rows:
        copy.wait()

    dwin[3 * BLK : 5 * BLK, :] = dot(ct[...], wv[3].reshape(D, HH)).astype(BF16)

    def around(first, count):
        return dwin.at[pl.ds(first * BLK, count * BLK)]

    halo = [
        remote(around(4, 1), around(2, 1), sd.at[0], rd.at[0], up),
        remote(around(3, 1), around(5, 1), sd.at[1], rd.at[1], down),
        remote(around(3, 1), around(1, 1), sd.at[2], rd.at[2], up),
        remote(around(4, 1), around(6, 1), sd.at[3], rd.at[3], down),
    ]
    for copy in halo:
        copy.start()
    farther = [
        remote(around(2, 1), around(0, 1), sd.at[4], rd.at[4], up),
        remote(around(5, 1), around(7, 1), sd.at[5], rd.at[5], down),
    ]
    for copy in edges[2:]:
        copy.wait_recv()

    def project(step, carry):
        at = pl.ds(pl.multiple_of(step * OWN, OWN), OWN)
        rows_in = tw[at, :]
        for m, ref in ((1, kh), (2, vh)):
            full = dot(rows_in, wv[m].reshape(D, HH)).astype(BF16)
            for h in range(HEADS):
                ref[h, at, 0:HD] = full[:, h * HD : (h + 1) * HD]
        return carry

    def queries(first, count):
        at = slice(first * BLK, (first + count) * BLK)
        full = dot(tw[at, :], wv[0].reshape(D, HH)).astype(BF16)
        for h in range(HEADS):
            qh[h, at, 0:HD] = full[:, h * HD : (h + 1) * HD]

    lax.fori_loop(0, 4, project, 0)
    queries(3, 2)
    for h in range(HEADS):
        dh[h, 3 * BLK : 5 * BLK, 0:HD] = dwin[3 * BLK : 5 * BLK, h * HD : (h + 1) * HD]
    halo[0].wait_recv()
    farther[0].start()
    halo[1].wait_recv()
    farther[1].start()

    lane = lax.broadcasted_iota(jnp.int32, (OWN, BLK), 1)
    stat[...] = jnp.zeros_like(stat)

    def ask_head(h, carry):
        k, v, d = kh[h], vh[h], dh[h, mine, :]
        s = dot_t(qh[h, mine, :], k) * SCALE2 + bias[...]
        top = jnp.max(s, axis=1, keepdims=True)
        e = jnp.exp2(s - top)
        norm = jnp.sum(e, axis=1, keepdims=True)
        p = e * (1.0 / norm)
        o = dot(p.astype(BF16), v).astype(BF16)
        oh[h] = o
        delta = jnp.sum(d.astype(F32) * o.astype(F32), axis=1, keepdims=True)
        ds = (p * (dot_t(d, v) - delta)).astype(BF16)
        gh[h] = (dot(ds, k) * SCALE).astype(BF16)
        lse = top + jnp.log2(norm)
        stat[...] = jnp.where(lane == h, lse, jnp.where(lane == h + HEADS, delta, stat[...]))
        return carry

    lax.fori_loop(0, HEADS, ask_head, 0)

    for i in range(2):
        sw[3 + i] = stat[i * BLK : (i + 1) * BLK, :].T[0 : 2 * HEADS, :]
    stats = [
        remote(sw.at[pl.ds(3, 2)], sw.at[pl.ds(1, 2)], st.at[0], rt.at[0], up),
        remote(sw.at[pl.ds(3, 2)], sw.at[pl.ds(5, 2)], st.at[1], rt.at[1], down),
        remote(sw.at[4], sw.at[0], st.at[2], rt.at[2], up2),
        remote(sw.at[3], sw.at[7], st.at[3], rt.at[3], down2),
    ]
    for copy in stats:
        copy.start()

    early = Wave(refs[0], sems[0], seq, x, y, core)
    late = Wave(refs[1], sems[1], seq, x, y, core)

    def partial(dst, lhs, rhs):
        def part(r, carry):
            at = pl.ds(pl.multiple_of(r * 352, 352), 352)
            full = dot(lhs[at, :], rhs[...])
            for k in range(4):
                dst[4 * r + k] = full[k * CHIP : (k + 1) * CHIP, :].astype(BF16)
            return carry

        lax.fori_loop(0, 4, part, 0)

    for h in range(HEADS):
        att[:, h * HD : (h + 1) * HD] = oh[h, :, 0:HD]
        dq[:, h * HD : (h + 1) * HD] = gh[h, :, 0:HD]
    partial(early.g.at[0], tok_t, dq)
    partial(early.g.at[1], cot_t, att)
    early.share()
    queries(0, 3)
    queries(5, 3)

    halo[2].wait_recv()
    halo[3].wait_recv()
    farther[0].wait_recv()
    farther[1].wait_recv()
    for h in range(HEADS):
        dh[h, 0 : 3 * BLK, 0:HD] = dwin[0 : 3 * BLK, h * HD : (h + 1) * HD]
        dh[h, 5 * BLK : 8 * BLK, 0:HD] = dwin[5 * BLK : 8 * BLK, h * HD : (h + 1) * HD]
    early.first(0)
    early.first(1)
    for copy in stats:
        copy.wait_recv()
    for i in range(8):
        rows[:, i * BLK : (i + 1) * BLK] = sw[i]

    def give_head(h, carry):
        q, d = qh[h], dh[h]
        lse = rows[pl.ds(h, 1), :]
        delta = rows[pl.ds(h + HEADS, 1), :]
        s = dot_t(kh[h, mine, :], q) * SCALE2 + bias2[...]
        p = jnp.exp2(s - lse)
        ds = (p * (dot_t(vh[h, mine, :], d) - delta)).astype(BF16)
        vg[h] = dot(p.astype(BF16), d).astype(BF16)
        kg[h] = (dot(ds, q) * SCALE).astype(BF16)
        return carry

    lax.fori_loop(0, 2, give_head, 0)
    early.first(2)
    early.first(3)
    early.middle(0)
    lax.fori_loop(2, 4, give_head, 0)
    early.middle(1)
    lax.fori_loop(4, 6, give_head, 0)
    early.middle(2)
    early.middle(3)
    lax.fori_loop(6, 8, give_head, 0)
    for h in range(HEADS):
        dk[:, h * HD : (h + 1) * HD] = kg[h, :, 0:HD]
        dv[:, h * HD : (h + 1) * HD] = vg[h, :, 0:HD]
    partial(late.g.at[0], tok_t, dk)
    partial(late.g.at[1], tok_t, dv)
    late.share()
    early.last(0)
    out[...] = dot_t(att[...], wv[3].reshape(D, HH)).astype(BF16)
    early.last(1)
    late.first(0)
    early.last(2)
    late.first(1)
    late.middle(0)
    early.last(3)
    late.first(2)
    late.middle(1)
    early.spread(total)
    late.first(3)
    late.middle(2)
    late.last(0)
    late.middle(3)
    late.last(1)
    early.finish()
    late.last(2)
    late.last(3)
    late.spread(total)
    early.pass_on()
    gin[...] = (
        dot_t(dq[...], wv[0].reshape(D, HH))
        + dot_t(dk[...], wv[1].reshape(D, HH))
        + dot_t(dv[...], wv[2].reshape(D, HH))
    ).astype(BF16)
    late.finish()
    early.collect(gout, 0, 3)
    late.pass_on()
    late.collect(gout, 1, 2)
    for copy in halo + farther + stats + edges + weights.sends + swaps:
        copy.wait_send()


def sublayer(wsh, tok, cot, cols, cuts, keep):
    dma = pltpu.SemaphoreType.DMA
    grid16 = (NX * NY, CHIP, HH)
    heads, heads_own = (HEADS, WINDOW, BLK), (HEADS, OWN, BLK)
    bf = lambda *shape: pltpu.VMEM(shape, BF16)
    scratch = [bf(4, *grid16), bf(WINDOW, D), bf(OWN, D)]
    scratch += [bf(*heads)] * 4 + [bf(*heads_own)] * 4
    scratch += [
        bf(WINDOW, HH),
        pltpu.VMEM((OWN, WINDOW), F32),
        pltpu.VMEM((OWN, WINDOW), F32),
        pltpu.VMEM((OWN, BLK), F32),
        pltpu.VMEM((8, 2 * HEADS, BLK), F32),
        pltpu.VMEM((2 * HEADS, WINDOW), F32),
        bf(D, OWN),
        bf(D, OWN),
    ]
    scratch += [bf(OWN, HH)] * 4 + [pltpu.VMEM((CHIP, HH), F32)]
    scratch += [bf(2, wsh.shape[1], HH), bf(2, CHIP, HH)]
    for wave in range(2):
        scratch += [
            bf(2, *grid16),
            bf(*grid16),
            bf(4, CHIP, HH),
            bf(4, 2, CHIP, HH),
            bf(3, CHIP, HH),
            bf(8, 24, 384),
            bf(7, 24, 384),
            bf(2, 8, 24, 384),
        ]
    scratch += [dma((4,))] + [dma((6,))] * 2 + [dma((4,))] * 2
    for wave in range(2):
        for count in (16, 16, 3, 7, 7, 8):
            scratch += [dma((count,))] * 2
    for count in (2, 6, 8, 32, 32):
        scratch += [dma((count,))] * 2
    return pl.pallas_call(
        sublayer_kernel,
        out_shape=(
            jax.ShapeDtypeStruct((OWN, D), BF16),
            jax.ShapeDtypeStruct((OWN, D), BF16),
            jax.ShapeDtypeStruct((4, CHIP, HH), F32),
        ),
        in_specs=[VMEM, HBM, HBM, SMEM, SMEM, VMEM],
        out_specs=(VMEM,) * 3,
        scratch_shapes=scratch,
        compiler_params=pltpu.CompilerParams(
            collective_id=1, has_side_effects=True, vmem_limit_bytes=62 << 20
        ),
        name="sublayer",
    )(wsh, tok, cot, cols, cuts, keep)


def body(tokens, weights, cotangent, col_list, cut_lengths, keep_mask):
    core = lax.axis_index("dp") % 2
    shard = weights.shape[0]
    result, grad_in, summed = sublayer(
        jnp.transpose(weights, (1, 0, 2)),
        tokens[0],
        cotangent[0],
        col_list[0].T,
        cut_lengths[0],
        keep_mask[0].reshape(NBLK, BLK),
    )
    mine = lax.dynamic_slice(summed, (0, shard * core, 0), (4, shard, HH))
    return (result[None], grad_in[None], jnp.transpose(mine, (1, 0, 2)))


def solution(mesh):
    placed = (
        P("dp", "seq", None),
        P("dp", None, None),
        P("dp", "seq", None),
        P("dp", None, None),
        P("dp", None),
        P("dp", None),
    )
    return jax.shard_map(
        body,
        mesh=mesh,
        in_specs=placed,
        out_specs=(P("dp", "seq", None), P("dp", "seq", None), P("dp", None, None)),
        check_vma=False,
    )
```
